256 devices in a mesh: pipe: 4 (over z_hi, core), expert: 64 (over x, y, z_lo).
Axes of the slice: x: 4, y: 4, z: 8 (z_hi: 2, z_lo: 4; z = z_hi * 4 + z_lo), core: 2. Of those that a mesh axis runs over, the one named last changes fastest.
Arguments:
- held: bfloat16 [4, 2048, 2048], P('pipe', 'expert'), may hold values from -23 to 23
- fresh: bfloat16 [2048, 2048], P('expert'), may hold values from -23 to 23
- routes: int32 [4, 2048, 2], P('pipe', 'expert'), may hold values from 0 to 7, all different within a row; in each aligned block of 32 rows (0 to 31, 32 to 63, ..., all dimensions but the last counted through in order) at most 16 rows name the same one
- norm_gain: float32 [4, 2048], P('pipe'), may hold values from 0.25 to 1.75
- router: bfloat16 [4, 2048, 8], P('pipe'), may hold values from -0.125 to 0.125
- w_gate: bfloat16 [4, 64, 2048, 896], P('pipe', 'expert'), may hold values from -0.125 to 0.125
- w_up: bfloat16 [4, 64, 2048, 896], P('pipe', 'expert'), may hold values from -0.125 to 0.125
- w_down: bfloat16 [4, 64, 896, 2048], P('pipe', 'expert'), may hold values from -0.0625 to 0.0625
Outputs:
- section_out: bfloat16 [4, 2048, 2048], P('pipe', 'expert')
The draws below stay inside these ranges and needn't reach their ends.
Inputs may be any that keep to these rules, and one draw needn't show every extreme that they name: `routes`: each token names two different experts; among the 32 tokens of one device at one section no expert is named more than 16 times, and in every draw some device's tokens name one expert exactly 16 times.
All inputs are finite; a program needn't handle non-finite values.
Results may differ from the reference program's by a relative error of at most 0.0045.
Values may be sent and summed in bfloat16 or wider, within the bound.
A program may use at most 128 MiB of HBM per device.

```python
import math
import jax
import jax.numpy as jnp
import numpy as np
from jax import lax

D = 2048
FF = 7168
EXPERTS = 8
TOP = 2
TOK_DEV = 32
SECTIONS = 4
SHARDS = 8
HID_DEV = 896
CAP = 16
TOKENS = 2048
N_EXPERT = 64


def scaled_rows(key, row_count):
    key_base = jax.random.fold_in(key, 11)
    key_rows = jax.random.fold_in(key, 12)
    key_cols = jax.random.fold_in(key, 13)
    base_draw = jnp.clip(jax.random.normal(key_base, (row_count, D), jnp.float32), -5.0, 5.0)
    row_scale = jnp.exp(jax.random.uniform(key_rows, (row_count, 1), jnp.float32, -0.92, 0.92))
    col_scale = jnp.exp(jax.random.uniform(key_cols, (1, D), jnp.float32, -0.6, 0.6))
    return base_draw * row_scale * col_scale


def draw_held(key, part):
    values = scaled_rows(jax.random.fold_in(key, 1), SECTIONS * TOKENS)
    return values.reshape(SECTIONS, TOKENS, D).astype(jnp.bfloat16)


def draw_fresh(key, part):
    return scaled_rows(jax.random.fold_in(key, 2), TOKENS).astype(jnp.bfloat16)


def shard_levels(own_key, shape, shards, low, largest):
    factor_of, own = 1.0, jax.random.fold_in(own_key, 6)
    for dim, shards_of in shards:
        heights = jnp.exp(jax.random.uniform(jax.random.fold_in(own, dim), (shards_of,), jnp.float32, low / len(shards), largest / len(shards)))
        factor_of = factor_of * jnp.repeat(heights, shape[dim] // shards_of).reshape([-1 if axis == dim else 1 for axis in range(len(shape))])
    return factor_of


def deal_out(stream_key, own, number, rows, number_of, top, reach, slope):
    sequence = jax.random.permutation(stream_key, number_of)
    packed, usual = load_shares(number_of, rows * top, reach, slope, True), load_shares(number_of, rows * top, reach, slope, False)
    places = jnp.arange(number_of)

    def named(lengths, rotation):
        used = int((lengths > 0).sum())
        fixed = max(1, used // 4)
        shifted = fixed + (places - fixed + rotation * (used - fixed)) % max(1, number_of - fixed)
        return jnp.zeros((number_of,), jnp.int32).at[sequence[jnp.where(places < fixed, places, shifted)]].set(jnp.asarray(lengths, jnp.int32))

    lengths = jnp.where(number % 4 == 0, named(packed, number // 4), named(usual, number - number // 4 - 1))
    mixed = jax.random.permutation(jax.random.fold_in(own, 3), number_of)
    donor, receiver = mixed[0:number_of // 2 * 2:2], mixed[1:number_of // 2 * 2:2]
    room = jnp.minimum(lengths[donor] - 1, reach - lengths[receiver]) // 2
    room = jnp.where((donor == sequence[0]) | (receiver == sequence[0]) | (lengths[receiver] == 0), 0, jnp.maximum(room, 0))
    shifted = jax.random.randint(jax.random.fold_in(own, 4), (number_of // 2,), 0, 1 << 20) % (room + 1)
    lengths = lengths.at[donor].add(-shifted).at[receiver].add(shifted)
    members = jnp.searchsorted(jnp.cumsum(lengths), jnp.arange(rows * top), side="right").astype(jnp.int32)
    grid = members.reshape(top, rows).T
    grid = grid[jax.random.permutation(jax.random.fold_in(own, 1), rows)]
    rotation = jax.random.randint(jax.random.fold_in(own, 2), (rows, 1), 0, top)
    return jnp.take_along_axis(grid, (jnp.arange(top)[None, :] + rotation) % top, axis=1)


def load_shares(count, total, reach, lean, full):
    weights = [(1 << 20) // math.isqrt(grade ** lean) + 1 for grade in range(1, count + 1)]
    largest = reach if full else min(reach, max(-(-total // count), total * weights[0] // sum(weights)))
    least = 1 if total - largest >= count - 1 else 0
    counts, surplus = [largest] + [least] * (count - 1), total - largest - least * (count - 1)
    while surplus > 0:
        candidates = [i for i in range(1, count) if counts[i] < largest] or [i for i in range(1, count) if counts[i] < reach]
        whole, budget = sum([weights[i] for i in candidates]), surplus
        for i in candidates:
            addition = min(reach - counts[i], max(1, budget * weights[i] // whole), surplus)
            counts[i] = counts[i] + addition
            surplus = surplus - addition
    return np.array(counts)


def centred(own_key, shape, deviation, bound, pieces=(), kind=jnp.bfloat16):
    values = jax.random.normal(own_key, shape, jnp.float32) * deviation
    if len(pieces) > 0:
        values = shard_levels(own_key, shape, pieces, -0.22, 0.18) * values
    return jnp.clip(values, min=-bound, max=bound).astype(kind)


def setup_inputs(seed: int = 0) -> dict:
    key_list = jax.random.split(jax.random.key(seed), 9)
    held = draw_held(jax.random.fold_in(key_list[8], 71), 0)
    fresh = draw_fresh(jax.random.fold_in(key_list[8], 71), 0)
    routes_keys = jax.random.split(jax.random.fold_in(key_list[2], 1), SECTIONS * TOKENS // TOK_DEV)
    routes_turns = jax.random.permutation(jax.random.fold_in(key_list[2], 3), SECTIONS * TOKENS // TOK_DEV)
    routes = jax.vmap(lambda own, number: deal_out(jax.random.fold_in(key_list[2], 2), own, number, TOK_DEV, EXPERTS, TOP, CAP, 2))(routes_keys, routes_turns).reshape((SECTIONS, TOKENS, TOP))
    norm_gain = jnp.clip(1.0 + 0.15 * jax.random.normal(key_list[3], (SECTIONS, D), jnp.float32), 0.25, 1.75)
    router = centred(key_list[4], (SECTIONS, D, EXPERTS), D ** -0.5, 0.125, ((0, 4),))
    w_gate = centred(key_list[5], (SECTIONS, N_EXPERT, D, HID_DEV), D ** -0.5, 0.125, ((0, 4), (1, 64)))
    w_up = centred(key_list[6], (SECTIONS, N_EXPERT, D, HID_DEV), D ** -0.5, 0.125, ((0, 4), (1, 64)))
    w_down = centred(key_list[7], (SECTIONS, N_EXPERT, HID_DEV, D), FF ** -0.5, 0.0625, ((0, 4), (1, 64)))
    return {"held": held, "fresh": fresh, "routes": routes, "norm_gain": norm_gain, "router": router, "w_gate": w_gate, "w_up": w_up, "w_down": w_down}


def rms_normed(values, gain):
    mean_square = lax.optimization_barrier(jnp.mean(values * values, axis=-1, keepdims=True))
    return (values * lax.rsqrt(mean_square + 1e-05) * gain).astype(jnp.bfloat16)

def reference(held, fresh, routes, norm_gain, router, w_gate, w_up, w_down):
    rows_cap = N_EXPERT * CAP
    outputs = []
    for section_number in range(SECTIONS):
        if section_number == 0:
            inputs = fresh
        else:
            inputs = held[section_number - 1]
        values = inputs.astype(jnp.float32)
        normed = rms_normed(values, norm_gain[section_number])
        logits = jnp.dot(normed, router[section_number], preferred_element_type=jnp.float32)
        chosen = routes[section_number].astype(jnp.int32)
        picked_logits = jnp.take_along_axis(logits, chosen, axis=1)
        shares = jnp.stack([jax.nn.sigmoid(picked_logits[:, 0] - picked_logits[:, 1]), jax.nn.sigmoid(picked_logits[:, 1] - picked_logits[:, 0])], axis=1)
        gate_all = w_gate[section_number].reshape(EXPERTS, SHARDS, D, HID_DEV)
        up_all = w_up[section_number].reshape(EXPERTS, SHARDS, D, HID_DEV)
        down_all = w_down[section_number].reshape(EXPERTS, SHARDS, HID_DEV, D)
        branch = jnp.zeros((TOKENS, D), jnp.float32)
        for expert_number in range(EXPERTS):
            hits = chosen == expert_number
            weight_share = lax.optimization_barrier(jnp.sum(jnp.where(hits, shares, jnp.zeros_like(shares)), axis=1))
            routed_mask = jnp.any(hits, axis=1)
            token_index = jnp.nonzero(routed_mask, size=rows_cap, fill_value=0)[0].astype(jnp.int32)
            routed_count = jnp.sum(routed_mask.astype(jnp.int32))
            live_rows = (jnp.arange(rows_cap, dtype=jnp.int32) < routed_count).astype(jnp.float32)
            picked_rows = normed[token_index]
            gate_matrix = jnp.transpose(gate_all[expert_number], (1, 0, 2)).reshape(D, FF)
            up_matrix = jnp.transpose(up_all[expert_number], (1, 0, 2)).reshape(D, FF)
            gate_proj = jnp.dot(picked_rows, gate_matrix, preferred_element_type=jnp.float32)
            up_proj = jnp.dot(picked_rows, up_matrix, preferred_element_type=jnp.float32)
            hidden = (jax.nn.silu(gate_proj) * up_proj).astype(jnp.bfloat16)
            partials = jnp.einsum('rsh,shd->srd', hidden.reshape(rows_cap, SHARDS, HID_DEV).astype(jnp.float32), down_all[expert_number].astype(jnp.float32)).astype(jnp.bfloat16)
            expert_out = lax.optimization_barrier(jnp.sum(partials.astype(jnp.float32), axis=0)).astype(jnp.bfloat16)
            expert_out = lax.optimization_barrier(expert_out).astype(jnp.float32)
            scaled = (weight_share[token_index] * live_rows)[:, None] * expert_out
            branch = branch.at[token_index].add(scaled)
        outputs.append((values + branch).astype(jnp.bfloat16))
    return jnp.stack(outputs)
```

```python
import functools

import jax
import jax.numpy as jnp
from jax import lax
from jax.experimental import pallas as pl
from jax.experimental.pallas import tpu as pltpu
from jax.sharding import PartitionSpec as P

MESH = pl.DeviceIdType.MESH
SIDE = 4
EXPERTS = 8
CAP = 16
TOK = 32
META = 128
BLOCK = SIDE * CAP
F32 = jnp.float32
BF16 = jnp.bfloat16


def passed_along(x, axis, by):
    length = lax.axis_size(axis)
    pairs = [(i, i + by) for i in range(length) if 0 <= i + by < length]
    return lax.ppermute(x, axis, pairs)


def z_partner(z, k):
    return (z, z + 1 - 2 * (z % 2), (z + 2) % SIDE, 3 - z)[k]


def moe_kernel(
    ext_ref, inputs_ref, gate_ref, up_ref, down_ref, out_ref,
    dense, slots, rows, parts, back, merged, spread, sums, final, hidden, w_in, w_out,
    z_send, z_recv, d_send, d_recv, f_send, f_recv,
    rf_send, rf_recv, rd_send, rd_recv, rz_send, rz_recv, w_sem,
):
    me = lax.axis_index("expert")
    x, y, z = me // 16, (me // 4) % 4, me % 4
    width = inputs_ref.shape[1]
    tiles = gate_ref.shape[1] // 128

    def at(nx, ny, nz):
        return {"expert": nx * 16 + ny * 4 + nz}

    def along(axis, by):
        if axis == "x":
            return at((x + by + SIDE) % SIDE, y, z)
        return at(x, (y + by + SIDE) % SIDE, z)

    inner = ("x", "y", "y", "x")
    outer = ("y", "x", "x", "y")

    barrier = pltpu.get_barrier_semaphore()
    for d in range(1, SIDE):
        for who in (along("x", d), along("y", d), at(x, y, z_partner(z, d))):
            pl.semaphore_signal(barrier, inc=1, device_id=who, device_id_type=MESH)
    pl.semaphore_wait(barrier, 9)

    def remote(src, dst, send, recv, who):
        return pltpu.make_async_remote_copy(
            src_ref=src, dst_ref=dst, send_sem=send, recv_sem=recv, device_id=who, device_id_type=MESH
        )

    z_copy = {
        k: remote(ext_ref, dense.at[k, 0], z_send.at[k], z_recv.at[k], at(x, y, z_partner(z, k)))
        for k in range(1, SIDE)
    }

    def d_copies(k):
        src = ext_ref if k == 0 else dense.at[k, 0]
        return [
            remote(src, dense.at[k, d], d_send.at[k, d], d_recv.at[k, d], along(inner[k], d))
            for d in range(1, SIDE)
        ]

    def f_copies(k):
        return [
            remote(slots.at[k, d - 1], rows.at[k, d], f_send.at[k, d], f_recv.at[k, d], along(outer[k], d))
            for d in range(1, SIDE)
        ]

    def rf_copies(k):
        return [
            remote(parts.at[k, d - 1], back.at[k, d], rf_send.at[k, d], rf_recv.at[k, d], along(outer[k], -d))
            for d in range(1, SIDE)
        ]

    def rd_copies(k):
        return [
            remote(merged.at[k, d], spread.at[k, d - 1], rd_send.at[k, d], rd_recv.at[k, d], along(inner[k], -d))
            for d in range(1, SIDE)
        ]

    rz_copy = {
        k: remote(sums.at[k], final.at[k], rz_send.at[k], rz_recv.at[k], at(x, y, z_partner(z, k)))
        for k in range(1, SIDE)
    }
    steps = {}

    def start(name, k, copies):
        steps[name, k] = copies
        for copy in copies:
            copy.start()

    def arrive(name, k):
        for copy in steps[name, k]:
            copy.wait_recv()

    def lane_expert(k, lane):
        block = lane // BLOCK
        if outer[k] == "y":
            return 2 * x + ((y + block) % SIDE) // 2
        return 2 * ((x + block) % SIDE) + y // 2

    def compact(k):
        tok = dense[k].reshape(SIDE * TOK, width + META)
        meta = tok[:, width:]
        lane = lax.broadcasted_iota(jnp.int32, (SIDE * BLOCK, META), 0)
        col = lax.broadcasted_iota(jnp.int32, (SIDE * BLOCK, META), 1)
        pick = (col == lane_expert(k, lane)).astype(F32).astype(BF16)
        found = lax.dot_general(pick, meta, (((1,), (1,)), ((), ())), preferred_element_type=F32)
        lane = lax.broadcasted_iota(jnp.int32, (SIDE * BLOCK, SIDE * TOK), 0)
        token = lax.broadcasted_iota(jnp.int32, (SIDE * BLOCK, SIDE * TOK), 1)
        want = (lane % CAP + 1).astype(F32)
        near = (lane % BLOCK) // CAP == token // TOK
        placing = jnp.where((found == want) & near, 1.0, 0.0).astype(BF16)
        moved = jnp.dot(placing, tok[:, :width], preferred_element_type=F32).astype(BF16)
        rows[k, 0] = moved[:BLOCK]
        slots[k] = moved[BLOCK:].reshape(SIDE - 1, BLOCK, width)

    def experts(k):
        taken = rows[k].reshape(SIDE * BLOCK, width)

        def first(n, carry):
            cols = pl.ds(pl.multiple_of(n * 256, 256), 256)
            both = jnp.dot(taken, w_in[:, cols], preferred_element_type=F32)
            gate, up = both[:, :128], both[:, 128:]
            value = gate / (1.0 + jnp.exp(-gate)) * up
            hidden[:, pl.ds(pl.multiple_of(n * 128, 128), 128)] = value.astype(BF16)
            return carry

        lax.fori_loop(0, tiles, first, 0)

        def second(n, carry):
            cols = pl.ds(pl.multiple_of(n * 256, 256), 256)
            value = jnp.dot(hidden[...], w_out[:, cols], preferred_element_type=F32).astype(BF16)
            back[k, 0, :, cols] = value[:BLOCK]
            for d in range(1, SIDE):
                parts[k, d - 1, :, cols] = value[d * BLOCK : (d + 1) * BLOCK]
            return carry

        lax.fori_loop(0, width // 256, second, 0)

    def merge(k):
        meta = dense[k, :, :, pl.ds(width, META)].reshape(SIDE * TOK, META)
        col = lax.broadcasted_iota(jnp.int32, (META, SIDE * BLOCK), 0)
        lane = lax.broadcasted_iota(jnp.int32, (META, SIDE * BLOCK), 1)
        mine = lane_expert(k, lane)

        def look(shift):
            pick = (col == mine + shift).astype(F32).astype(BF16)
            return jnp.dot(meta, pick, preferred_element_type=F32)

        token = lax.broadcasted_iota(jnp.int32, (SIDE * TOK, SIDE * BLOCK), 0)
        lane = lax.broadcasted_iota(jnp.int32, (SIDE * TOK, SIDE * BLOCK), 1)
        want = (lane % CAP + 1).astype(F32)
        near = (lane % BLOCK) // CAP == token // TOK
        match = (look(0) == want) & near
        high = jnp.where(match, look(EXPERTS), 0.0).astype(BF16)
        low = jnp.where(match, look(2 * EXPERTS), 0.0).astype(BF16)
        came = back[k].reshape(SIDE * BLOCK, width)
        total = jnp.dot(high, came, preferred_element_type=F32) + jnp.dot(low, came, preferred_element_type=F32)
        merged[k] = total.astype(BF16).reshape(SIDE, TOK, width)

    def gather_sum(k):
        total = merged[k, 0].astype(F32)
        for d in range(1, SIDE):
            total = total + spread[k, d - 1].astype(F32)
        sums[k] = total.astype(BF16)

    weights = [pltpu.make_async_copy(down_ref, w_out, w_sem.at[2 * tiles])]
    for n in range(tiles):
        for j, ref in enumerate((gate_ref, up_ref)):
            weights.append(
                pltpu.make_async_copy(
                    ref.at[:, pl.ds(n * 128, 128)],
                    w_in.at[:, pl.ds(n * 256 + j * 128, 128)],
                    w_sem.at[2 * n + j],
                )
            )

    order = (0, 2, 3, 1)
    start("d", 0, d_copies(0))
    for k in order[1:]:
        start("z", k, [z_copy[k]])
    for copy in weights:
        copy.start()
    dense[0, 0] = ext_ref[...]

    def dense_on(k):
        arrive("z", k)
        start("d", k, d_copies(k))

    def dispatch(k):
        arrive("d", k)
        compact(k)
        start("f", k, f_copies(k))

    def compute(k):
        arrive("f", k)
        experts(k)
        start("rf", k, rf_copies(k))

    def combine(k):
        arrive("rf", k)
        merge(k)
        start("rd", k, rd_copies(k))

    def collect(k):
        arrive("rd", k)
        gather_sum(k)
        if k:
            start("rz", k, [rz_copy[k]])

    dense_on(2)
    dispatch(0)
    dense_on(3)
    dispatch(2)
    dense_on(1)
    dispatch(3)
    dispatch(1)
    for copy in weights:
        copy.wait()
    compute(0)
    compute(2)
    compute(3)
    combine(0)
    compute(1)
    combine(2)
    collect(0)
    collect(2)
    combine(3)
    combine(1)
    collect(3)
    collect(1)
    total = inputs_ref[...].astype(F32) + sums[0].astype(F32)
    for k in order[1:]:
        arrive("rz", k)
        total = total + final[k].astype(F32)
    out_ref[...] = total.astype(BF16)
    for copies in steps.values():
        for copy in copies:
            copy.wait_send()


def run_layer(ext, inputs, gate, up, down):
    tok, width = inputs.shape
    hid = gate.shape[1]
    vmem = pl.BlockSpec(memory_space=pltpu.VMEM)
    hbm = pl.BlockSpec(memory_space=pl.ANY)
    dma = pltpu.SemaphoreType.DMA
    pairs = [dma((SIDE,)), dma((SIDE,))]
    grids = [dma((SIDE, SIDE)), dma((SIDE, SIDE))]
    return pl.pallas_call(
        moe_kernel,
        out_shape=jax.ShapeDtypeStruct((tok, width), BF16),
        in_specs=[vmem, vmem, hbm, hbm, hbm],
        out_specs=vmem,
        scratch_shapes=[
            pltpu.VMEM((SIDE, SIDE, tok, width + META), BF16),
            pltpu.VMEM((SIDE, SIDE - 1, BLOCK, width), BF16),
            pltpu.VMEM((SIDE, SIDE, BLOCK, width), BF16),
            pltpu.VMEM((SIDE, SIDE - 1, BLOCK, width), BF16),
            pltpu.VMEM((SIDE, SIDE, BLOCK, width), BF16),
            pltpu.VMEM((SIDE, SIDE, tok, width), BF16),
            pltpu.VMEM((SIDE, SIDE - 1, tok, width), BF16),
            pltpu.VMEM((SIDE, tok, width), BF16),
            pltpu.VMEM((SIDE, tok, width), BF16),
            pltpu.VMEM((SIDE * BLOCK, hid), BF16),
            pltpu.VMEM((width, 2 * hid), BF16),
            pltpu.VMEM((hid, width), BF16),
        ]
        + pairs + grids + grids + grids + grids + pairs
        + [dma((2 * (hid // 128) + 1,))],
        compiler_params=pltpu.CompilerParams(
            collective_id=0, has_side_effects=True, vmem_limit_bytes=60 * 1024 * 1024
        ),
        name="moe_relay",
    )(ext, inputs, gate, up, down)


def per_device(held, fresh, routes, norm_gain, router, w_gate, w_up, w_down):
    received = passed_along(held[0], "pipe", 1)
    section_index = lax.axis_index("pipe")
    inputs = jnp.where(section_index == 0, fresh, received)
    values = inputs.astype(F32)
    mean_square = jnp.mean(values * values, axis=-1, keepdims=True)
    normed = (values * lax.rsqrt(mean_square + 1e-05) * norm_gain[0]).astype(BF16)
    logits = jnp.dot(normed, router[0], preferred_element_type=F32)
    chosen = routes[0]
    expert_ids = jnp.arange(EXPERTS, dtype=jnp.int32)
    hits = chosen[:, :, None] == expert_ids[None, None, :]
    picked = jnp.sum(hits.astype(F32) * logits[:, None, :], axis=2)
    share = jax.nn.sigmoid(picked - picked[:, ::-1])
    weight = jnp.sum(hits.astype(F32) * share[:, :, None], axis=1)
    high = lax.reduce_precision(weight, 8, 7)
    low = weight - high
    hit = jnp.any(hits, axis=1).astype(F32)
    earlier = jnp.tril(jnp.ones((TOK, TOK), F32))
    slot = hit * jnp.dot(earlier, hit, preferred_element_type=F32)
    pad = jnp.zeros((TOK, META - 3 * EXPERTS), BF16)
    ext = jnp.concatenate(
        [normed, slot.astype(BF16), high.astype(BF16), low.astype(BF16), pad], axis=1
    )
    out = run_layer(ext, inputs, w_gate[0, 0], w_up[0, 0], w_down[0, 0])
    return out[None]


def solution(mesh):
    in_specs = (
        P("pipe", "expert", None),
        P("expert", None),
        P("pipe", "expert", None),
        P("pipe", None),
        P("pipe", None, None),
        P("pipe", "expert", None, None),
        P("pipe", "expert", None, None),
        P("pipe", "expert", None, None),
    )
    out_specs = P("pipe", "expert", None)
    return jax.shard_map(
        per_device, mesh=mesh, in_specs=in_specs, out_specs=out_specs, check_vma=False
    )
```

```python
import functools

import jax
import jax.numpy as jnp
from jax import lax
from jax.experimental import pallas as pl
from jax.experimental.pallas import tpu as pltpu
from jax.sharding import PartitionSpec as P

MESH = pl.DeviceIdType.MESH
SIDE = 4
EXPERTS = 8
CAP = 16
TOK = 32
META = 128
BLOCK = SIDE * CAP
F32 = jnp.float32
BF16 = jnp.bfloat16


def z_partner(z, k):
    return (z, z + 1 - 2 * (z % 2), (z + 2) % SIDE, 3 - z)[k]


def moe_kernel(
    held_ref, fresh_ref, routes_ref, gain_ref, router_ref, gate_ref, up_ref, down_ref, out_ref,
    inputs, dense, slots, rows, parts, back, merged, spread, sums, final, pair_parts, pair_merged, hidden, w_in, w_out,
    z_send, z_recv, d_send, d_recv, f_send, f_recv,
    rf_send, rf_recv, rd_send, rd_recv, rz_send, rz_recv, q_send, q_recv, p_send, p_recv, w_sem,
):
    me = lax.axis_index("expert")
    stage, stages = lax.axis_index("pipe"), lax.axis_size("pipe")
    x, y, z = me // 16, (me // 4) % 4, me % 4
    width = fresh_ref.shape[1]
    tiles = gate_ref.shape[1] // 128

    def at(nx, ny, nz):
        return {"expert": nx * 16 + ny * 4 + nz}

    def along(axis, by):
        if axis == "x":
            return at((x + by + SIDE) % SIDE, y, z)
        return at(x, (y + by + SIDE) % SIDE, z)

    inner = ("x", "x", "y", "y")
    outer = ("y", "y", "x", "x")

    def section(by):
        return {"pipe": stage + by, "expert": me}

    barrier = pltpu.get_barrier_semaphore()

    @pl.when(stage < stages - 1)
    def _():
        pl.semaphore_signal(barrier, inc=1, device_id=section(1), device_id_type=MESH)

    @pl.when(stage > 0)
    def _():
        pl.semaphore_signal(barrier, inc=1, device_id=section(-1), device_id_type=MESH)

    for d in range(1, SIDE):
        for who in (along("x", d), along("y", d), at(x, y, z_partner(z, d))):
            pl.semaphore_signal(barrier, inc=1, device_id=who, device_id_type=MESH)
    before, after = (stage + stages - 1) // stages, (2 * stages - 2 - stage) // stages
    pl.semaphore_wait(barrier, 9 + before + after)

    def remote(src, dst, send, recv, who):
        return pltpu.make_async_remote_copy(
            src_ref=src, dst_ref=dst, send_sem=send, recv_sem=recv, device_id=who, device_id_type=MESH
        )

    relay = remote(held_ref, inputs, p_send.at[0], p_recv.at[0], section(1))

    @pl.when(stage < stages - 1)
    def _():
        relay.start()

    z_copy = {
        k: remote(dense.at[0, 0], dense.at[k, 0], z_send.at[k], z_recv.at[k], at(x, y, z_partner(z, k)))
        for k in range(1, SIDE)
    }

    def d_copies(k):
        return {
            d: remote(dense.at[k, 0], dense.at[k, d], d_send.at[k, d], d_recv.at[k, d], along(inner[k], d))
            for d in near_hops(k)
        }

    def f_copies(k):
        return {
            d: remote(slots.at[k, d - 1], rows.at[k, d], f_send.at[k, d], f_recv.at[k, d], along(outer[k], d))
            for d in near_hops(k)
        }

    def rf_copies(k):
        return {
            d: remote(parts.at[k, d - 1], back.at[k, d], rf_send.at[k, d], rf_recv.at[k, d], along(outer[k], -d))
            for d in near_hops(k ^ 1)
        }

    def rd_copies(k):
        return {
            d: remote(merged.at[k, d], spread.at[k, d - 1], rd_send.at[k, d], rd_recv.at[k, d], along(inner[k], -d))
            for d in near_hops(k ^ 1)
        }

    def near_hops(k):
        return (2, 1, 3) if k % 2 == 0 else (1, 3)

    twin = at(x, y, z_partner(z, 1))

    def pair_copy(kind, src, dst, k):
        return {0: remote(src, dst, q_send.at[kind, k // 2], q_recv.at[kind, k // 2], twin)}

    rz_copy = {
        k: remote(sums.at[k], final.at[k], rz_send.at[k], rz_recv.at[k], at(x, y, z_partner(z, k)))
        for k in range(1, SIDE)
    }
    steps = {}

    def start(name, k, copies):
        steps[name, k] = copies
        for copy in copies.values():
            copy.start()

    def arrive(name, k, hops=None):
        for d, copy in steps[name, k].items():
            if hops is None or d in hops:
                copy.wait_recv()

    def lane_expert(k, lane):
        block = lane // BLOCK
        if outer[k] == "y":
            return 2 * x + ((y + block) % SIDE) // 2
        return 2 * ((x + block) % SIDE) + y // 2

    def prepare():
        values = inputs[...].astype(F32)
        mean_square = jnp.mean(values * values, axis=-1, keepdims=True)
        normed = (values * lax.rsqrt(mean_square + 1e-05) * gain_ref[...]).astype(BF16)
        dense[0, 0, :, pl.ds(0, width)] = normed
        logits = lax.dot_general(
            router_ref[...], normed, (((1,), (1,)), ((), ())), preferred_element_type=F32
        )
        ids = lax.broadcasted_iota(jnp.int32, (EXPERTS, TOK), 0)
        first, second = ids == routes_ref[0:1, :], ids == routes_ref[1:2, :]
        gap = jnp.sum(jnp.where(first, logits, 0.0), axis=0, keepdims=True) - jnp.sum(
            jnp.where(second, logits, 0.0), axis=0, keepdims=True
        )
        share_a, share_b = 1.0 / (1.0 + jnp.exp(-gap)), 1.0 / (1.0 + jnp.exp(gap))
        weight = jnp.where(first, share_a, 0.0) + jnp.where(second, share_b, 0.0)
        high = weight.astype(BF16).astype(F32)
        hit = jnp.where(first | second, 1.0, 0.0)
        here = lax.broadcasted_iota(jnp.int32, (TOK, TOK), 0)
        there = lax.broadcasted_iota(jnp.int32, (TOK, TOK), 1)
        upto = jnp.where(here <= there, 1.0, 0.0).astype(BF16)
        slot = hit * jnp.dot(hit.astype(BF16), upto, preferred_element_type=F32)
        table = jnp.concatenate(
            [slot, high, weight - high, jnp.zeros((META - 3 * EXPERTS, TOK), F32)], axis=0
        ).astype(BF16)
        same = jnp.where(here == there, 1.0, 0.0).astype(BF16)
        meta = lax.dot_general(same, table, (((1,), (1,)), ((), ())), preferred_element_type=F32)
        dense[0, 0, :, pl.ds(width, META)] = meta.astype(BF16)

    def compact(k):
        tok = dense[k].reshape(SIDE * TOK, width + META)
        meta = tok[:, width:]
        lane = lax.broadcasted_iota(jnp.int32, (SIDE * BLOCK, META), 0)
        col = lax.broadcasted_iota(jnp.int32, (SIDE * BLOCK, META), 1)
        pick = (col == lane_expert(k, lane)).astype(F32).astype(BF16)
        found = lax.dot_general(pick, meta, (((1,), (1,)), ((), ())), preferred_element_type=F32)
        lane = lax.broadcasted_iota(jnp.int32, (SIDE * BLOCK, SIDE * TOK), 0)
        token = lax.broadcasted_iota(jnp.int32, (SIDE * BLOCK, SIDE * TOK), 1)
        want = (lane % CAP + 1).astype(F32)
        near = (lane % BLOCK) // CAP == token // TOK
        placing = jnp.where((found == want) & near, 1.0, 0.0).astype(BF16)
        moved = jnp.dot(placing, tok[:, :width], preferred_element_type=F32).astype(BF16)
        rows[k, 0] = moved[:BLOCK]
        slots[k] = moved[BLOCK:].reshape(SIDE - 1, BLOCK, width)

    def experts(k):
        taken = rows[k].reshape(SIDE * BLOCK, width)

        def first(n, carry):
            cols = pl.ds(pl.multiple_of(n * 256, 256), 256)
            both = jnp.dot(taken, w_in[:, cols], preferred_element_type=F32)
            gate, up = both[:, :128], both[:, 128:]
            value = gate / (1.0 + jnp.exp(-gate)) * up
            hidden[:, pl.ds(pl.multiple_of(n * 128, 128), 128)] = value.astype(BF16)
            return carry

        lax.fori_loop(0, tiles, first, 0)

        def second(n, carry):
            cols = pl.ds(pl.multiple_of(n * 256, 256), 256)
            value = jnp.dot(hidden[...], w_out[:, cols], preferred_element_type=F32)
            back[k, 0, :, cols] = value[:BLOCK].astype(BF16)
            for d in range(1, SIDE):
                part = value[d * BLOCK : (d + 1) * BLOCK]
                if d == 2 and k % 2:
                    part = part + pair_parts[k // 2, :, cols].astype(F32)
                parts[k, d - 1, :, cols] = part.astype(BF16)
            return carry

        lax.fori_loop(0, width // 256, second, 0)

    def merge(k):
        meta = dense[k, :, :, pl.ds(width, META)].reshape(SIDE * TOK, META)
        col = lax.broadcasted_iota(jnp.int32, (META, SIDE * BLOCK), 0)
        lane = lax.broadcasted_iota(jnp.int32, (META, SIDE * BLOCK), 1)
        mine = lane_expert(k, lane)

        def look(shift):
            pick = (col == mine + shift).astype(F32).astype(BF16)
            return jnp.dot(meta, pick, preferred_element_type=F32)

        token = lax.broadcasted_iota(jnp.int32, (SIDE * TOK, SIDE * BLOCK), 0)
        lane = lax.broadcasted_iota(jnp.int32, (SIDE * TOK, SIDE * BLOCK), 1)
        want = (lane % CAP + 1).astype(F32)
        near = (lane % BLOCK) // CAP == token // TOK
        match = (look(0) == want) & near
        high = jnp.where(match, look(EXPERTS), 0.0).astype(BF16)
        low = jnp.where(match, look(2 * EXPERTS), 0.0).astype(BF16)
        came = back[k].reshape(SIDE * BLOCK, width)
        total = jnp.dot(high, came, preferred_element_type=F32) + jnp.dot(low, came, preferred_element_type=F32)
        for d in range(SIDE):
            part = total[d * TOK : (d + 1) * TOK]
            if d == 2 and k % 2:
                part = part + pair_merged[k // 2].astype(F32)
            merged[k, d] = part.astype(BF16)

    def gather_sum(k):
        total = merged[k, 0].astype(F32)
        for d in near_hops(k ^ 1):
            total = total + spread[k, d - 1].astype(F32)
        sums[k] = total.astype(BF16)

    weights = [pltpu.make_async_copy(down_ref, w_out, w_sem.at[2 * tiles])]
    for n in range(tiles):
        for j, ref in enumerate((gate_ref, up_ref)):
            weights.append(
                pltpu.make_async_copy(
                    ref.at[:, pl.ds(n * 128, 128)],
                    w_in.at[:, pl.ds(n * 256 + j * 128, 128)],
                    w_sem.at[2 * n + j],
                )
            )

    for copy in weights:
        copy.start()

    @pl.when(stage == 0)
    def _():
        inputs[...] = fresh_ref[...]

    @pl.when(stage > 0)
    def _():
        relay.wait_recv()

    prepare()
    start("d", 0, d_copies(0))
    for k in (2, 1, 3):
        start("z", k, {0: z_copy[k]})
    for k in (0, 2):
        back[k, 2] = jnp.zeros((BLOCK, width), BF16)

    def dense_on(k):
        arrive("z", k)
        start("d", k, d_copies(k))

    def dispatch(k):
        arrive("d", k, (2,))
        if k % 2 == 0:
            start("zd", k, pair_copy(0, dense.at[k, 2], dense.at[k + 1, 2], k))
        else:
            arrive("zd", k - 1)
        arrive("d", k, (1, 3))
        compact(k)
        start("f", k, f_copies(k))

    def pass_rows(k):
        arrive("f", k, (2,))
        start("zf", k, pair_copy(1, rows.at[k, 2], rows.at[k + 1, 2], k))

    def compute(k):
        arrive("f", k, (1, 3))
        if k % 2:
            arrive("zf", k - 1)
            arrive("zrf", k - 1)
        experts(k)
        if k % 2 == 0:
            start("zrf", k, pair_copy(2, parts.at[k, 1], pair_parts.at[k // 2], k))
        start("rf", k, rf_copies(k))

    def combine(k):
        arrive("rf", k)
        if k % 2:
            arrive("zrd", k - 1)
        merge(k)
        if k % 2 == 0:
            start("zrd", k, pair_copy(3, merged.at[k, 2], pair_merged.at[k // 2], k))
        start("rd", k, rd_copies(k))

    def collect(k):
        arrive("rd", k)
        gather_sum(k)
        if k:
            start("rz", k, {0: rz_copy[k]})

    dense_on(2)
    dispatch(0)
    dense_on(1)
    dispatch(2)
    dense_on(3)
    dispatch(1)
    dispatch(3)
    pass_rows(0)
    pass_rows(2)
    for copy in weights:
        copy.wait()
    compute(0)
    compute(2)
    compute(1)
    combine(0)
    compute(3)
    combine(2)
    combine(1)
    combine(3)
    collect(0)
    collect(2)
    collect(3)
    collect(1)
    total = inputs[...].astype(F32) + sums[0].astype(F32)
    for k in (2, 3, 1):
        arrive("rz", k)
        total = total + final[k].astype(F32)
    out_ref[...] = total.astype(BF16)
    for copies in steps.values():
        for copy in copies.values():
            copy.wait_send()

    @pl.when(stage < stages - 1)
    def _():
        relay.wait_send()


def run_layer(held, fresh, routes, gain, router, gate, up, down):
    tok, width = fresh.shape
    hid = gate.shape[1]
    vmem = pl.BlockSpec(memory_space=pltpu.VMEM)
    hbm = pl.BlockSpec(memory_space=pl.ANY)
    dma = pltpu.SemaphoreType.DMA
    pairs = [dma((SIDE,)), dma((SIDE,))]
    grids = [dma((SIDE, SIDE)), dma((SIDE, SIDE))]
    return pl.pallas_call(
        moe_kernel,
        out_shape=jax.ShapeDtypeStruct((tok, width), BF16),
        in_specs=[hbm, vmem, vmem, vmem, vmem, hbm, hbm, hbm],
        out_specs=vmem,
        scratch_shapes=[
            pltpu.VMEM((tok, width), BF16),
            pltpu.VMEM((SIDE, SIDE, tok, width + META), BF16),
            pltpu.VMEM((SIDE, SIDE - 1, BLOCK, width), BF16),
            pltpu.VMEM((SIDE, SIDE, BLOCK, width), BF16),
            pltpu.VMEM((SIDE, SIDE - 1, BLOCK, width), BF16),
            pltpu.VMEM((SIDE, SIDE, BLOCK, width), BF16),
            pltpu.VMEM((SIDE, SIDE, tok, width), BF16),
            pltpu.VMEM((SIDE, SIDE - 1, tok, width), BF16),
            pltpu.VMEM((SIDE, tok, width), BF16),
            pltpu.VMEM((SIDE, tok, width), BF16),
            pltpu.VMEM((2, BLOCK, width), BF16),
            pltpu.VMEM((2, tok, width), BF16),
            pltpu.VMEM((SIDE * BLOCK, hid), BF16),
            pltpu.VMEM((width, 2 * hid), BF16),
            pltpu.VMEM((hid, width), BF16),
        ]
        + pairs + grids + grids + grids + grids + pairs
        + grids + [dma((1,)), dma((1,)), dma((2 * (hid // 128) + 1,))],
        compiler_params=pltpu.CompilerParams(
            collective_id=0, has_side_effects=True, vmem_limit_bytes=60 * 1024 * 1024
        ),
        name="moe_relay",
    )(held, fresh, routes, gain, router, gate, up, down)


def per_device(held, fresh, routes, norm_gain, router, w_gate, w_up, w_down):
    out = run_layer(
        held[0], fresh, routes[0].T, norm_gain, router[0].T, w_gate[0, 0], w_up[0, 0], w_down[0, 0]
    )
    return out[None]


def solution(mesh):
    in_specs = (
        P("pipe", "expert", None),
        P("expert", None),
        P("pipe", "expert", None),
        P("pipe", None),
        P("pipe", None, None),
        P("pipe", "expert", None, None),
        P("pipe", "expert", None, None),
        P("pipe", "expert", None, None),
    )
    out_specs = P("pipe", "expert", None)
    return jax.shard_map(
        per_device, mesh=mesh, in_specs=in_specs, out_specs=out_specs, check_vma=False
    )
```

```python
import functools

import jax
import jax.numpy as jnp
from jax import lax
from jax.experimental import pallas as pl
from jax.experimental.pallas import tpu as pltpu
from jax.sharding import PartitionSpec as P

MESH = pl.DeviceIdType.MESH
SIDE = 4
EXPERTS = 8
CAP = 16
TOK = 32
META = 128
BLOCK = SIDE * CAP
F32 = jnp.float32
BF16 = jnp.bfloat16


def z_partner(z, k):
    return (z, z + 1 - 2 * (z % 2), (z + 2) % SIDE, 3 - z)[k]


def moe_kernel(
    held_ref, fresh_ref, routes_ref, gain_ref, router_ref, gate_ref, up_ref, down_ref, out_ref,
    inputs, chosen, gain, router, dense, slots, rows, parts, back, merged, spread, sums, final, pair_parts, pair_merged, choice, hidden, w_in, w_out,
    z_send, z_recv, d_send, d_recv, f_send, f_recv,
    rf_send, rf_recv, rd_send, rd_recv, rz_send, rz_recv, q_send, q_recv, p_send, p_recv, i_sem, w_sem,
):
    me = lax.axis_index("expert")
    stage, stages = lax.axis_index("pipe"), lax.axis_size("pipe")
    x, y, z = me // 16, (me // 4) % 4, me % 4
    width = fresh_ref.shape[1]
    tiles = gate_ref.shape[1] // 128

    def at(nx, ny, nz):
        return {"expert": nx * 16 + ny * 4 + nz}

    def along(axis, by):
        if axis == "x":
            return at((x + by + SIDE) % SIDE, y, z)
        return at(x, (y + by + SIDE) % SIDE, z)

    inner = ("x", "x", "y", "y")
    outer = ("y", "y", "x", "x")

    def section(by):
        return {"pipe": stage + by, "expert": me}

    loads = [
        pltpu.make_async_copy(ref, to, i_sem.at[n])
        for n, (ref, to) in enumerate(((routes_ref, chosen), (gain_ref, gain), (router_ref, router)))
    ]
    for copy in loads:
        copy.start()
    first_tile = pltpu.make_async_copy(fresh_ref, inputs, i_sem.at[3])

    @pl.when(stage == 0)
    def _():
        first_tile.start()

    barrier = pltpu.get_barrier_semaphore()

    @pl.when(stage < stages - 1)
    def _():
        pl.semaphore_signal(barrier, inc=1, device_id=section(1), device_id_type=MESH)

    @pl.when(stage > 0)
    def _():
        pl.semaphore_signal(barrier, inc=1, device_id=section(-1), device_id_type=MESH)

    for d in range(1, SIDE):
        for who in (along("x", d), along("y", d), at(x, y, z_partner(z, d))):
            pl.semaphore_signal(barrier, inc=1, device_id=who, device_id_type=MESH)
    before, after = (stage + stages - 1) // stages, (2 * stages - 2 - stage) // stages
    pl.semaphore_wait(barrier, 9 + before + after)

    def remote(src, dst, send, recv, who):
        return pltpu.make_async_remote_copy(
            src_ref=src, dst_ref=dst, send_sem=send, recv_sem=recv, device_id=who, device_id_type=MESH
        )

    relay = remote(held_ref, inputs, p_send.at[0], p_recv.at[0], section(1))

    @pl.when(stage < stages - 1)
    def _():
        relay.start()

    z_copy = {
        k: remote(dense.at[0, 0], dense.at[k, 0], z_send.at[k], z_recv.at[k], at(x, y, z_partner(z, k)))
        for k in range(1, SIDE)
    }

    def d_copies(k):
        return {
            d: remote(dense.at[k, 0], dense.at[k, d], d_send.at[k, d], d_recv.at[k, d], along(inner[k], d))
            for d in near_hops(k)
        }

    def f_copies(k, low, high):
        span, lane = pl.ds(low * CAP, (high - low) * CAP), SIDE if low else 0
        return {
            d: remote(
                slots.at[k, d - 1, span], rows.at[k, d, span],
                f_send.at[k, lane + d], f_recv.at[k, lane + d], along(outer[k], d),
            )
            for d in near_hops(k)
        }

    def half(h):
        return pl.ds(h * (width // 2), width // 2)

    def rf_copies(k, h):
        return {
            d: remote(
                parts.at[k, d - 1, :, half(h)], back.at[k, d, :, half(h)],
                rf_send.at[k, h * SIDE + d], rf_recv.at[k, h * SIDE + d], along(outer[k], -d),
            )
            for d in near_hops(k ^ 1)
        }

    def rd_copies(k, h):
        return {
            d: remote(
                merged.at[k, d, :, half(h)], spread.at[k, d - 1, :, half(h)],
                rd_send.at[k, h * SIDE + d], rd_recv.at[k, h * SIDE + d], along(inner[k], -d),
            )
            for d in near_hops(k ^ 1)
        }

    def near_hops(k):
        return (2, 1, 3) if k % 2 == 0 else (1, 3)

    twin = at(x, y, z_partner(z, 1))

    def pair_copy(kind, src, dst, k, h=0):
        lane = h * SIDE + k // 2
        return {0: remote(src, dst, q_send.at[kind, lane], q_recv.at[kind, lane], twin)}

    def rz_copy(k, h):
        return remote(
            sums.at[k, :, half(h)], final.at[k, :, half(h)],
            rz_send.at[k, h], rz_recv.at[k, h], at(x, y, z_partner(z, k)),
        )

    steps = {}

    def start(name, k, copies):
        steps[name, k] = copies
        for copy in copies.values():
            copy.start()

    def arrive(name, k, hops=None):
        for d, copy in steps[name, k].items():
            if hops is None or d in hops:
                copy.wait_recv()

    def lane_expert(k, block):
        if outer[k] == "y":
            return 2 * x + ((y + block) % SIDE) // 2
        return 2 * ((x + block) % SIDE) + y // 2

    def prepare():
        values = inputs[...].astype(F32)
        mean_square = jnp.mean(values * values, axis=-1, keepdims=True)
        normed = (values * lax.rsqrt(mean_square + 1e-05) * gain[...]).astype(BF16)
        dense[0, 0, :, pl.ds(0, width)] = normed
        logits = lax.dot_general(
            router[...], normed, (((1,), (1,)), ((), ())), preferred_element_type=F32
        )
        ids = lax.broadcasted_iota(jnp.int32, (EXPERTS, TOK), 0)
        first, second = ids == chosen[0:1, :], ids == chosen[1:2, :]
        gap = jnp.sum(jnp.where(first, logits, 0.0), axis=0, keepdims=True) - jnp.sum(
            jnp.where(second, logits, 0.0), axis=0, keepdims=True
        )
        share_a, share_b = 1.0 / (1.0 + jnp.exp(-gap)), 1.0 / (1.0 + jnp.exp(gap))
        weight = jnp.where(first, share_a, 0.0) + jnp.where(second, share_b, 0.0)
        high = weight.astype(BF16).astype(F32)
        hit = jnp.where(first | second, 1.0, 0.0)
        here = lax.broadcasted_iota(jnp.int32, (TOK, TOK), 0)
        there = lax.broadcasted_iota(jnp.int32, (TOK, TOK), 1)
        upto = jnp.where(here <= there, 1.0, 0.0).astype(BF16)
        slot = hit * jnp.dot(hit.astype(BF16), upto, preferred_element_type=F32)
        table = jnp.concatenate(
            [slot, high, weight - high, jnp.zeros((META - 3 * EXPERTS, TOK), F32)], axis=0
        ).astype(BF16)
        same = jnp.where(here == there, 1.0, 0.0).astype(BF16)
        meta = lax.dot_general(same, table, (((1,), (1,)), ((), ())), preferred_element_type=F32)
        dense[0, 0, :, pl.ds(width, META)] = meta.astype(BF16)

    def compact(k, low, high):
        count, span = high - low, (high - low) * CAP
        tok = dense[k, low:high].reshape(count * TOK, width + META)
        meta = tok[:, width:]
        lane = lax.broadcasted_iota(jnp.int32, (SIDE * span, META), 0)
        col = lax.broadcasted_iota(jnp.int32, (SIDE * span, META), 1)
        pick = (col == lane_expert(k, lane // span)).astype(F32).astype(BF16)
        found = lax.dot_general(pick, meta, (((1,), (1,)), ((), ())), preferred_element_type=F32)
        lane = lax.broadcasted_iota(jnp.int32, (SIDE * span, count * TOK), 0)
        token = lax.broadcasted_iota(jnp.int32, (SIDE * span, count * TOK), 1)
        want = (lane % CAP + 1).astype(F32)
        near = (lane % span) // CAP == token // TOK
        placing = jnp.where((found == want) & near, 1.0, 0.0).astype(BF16)
        moved = jnp.dot(placing, tok[:, :width], preferred_element_type=F32).astype(BF16)
        rows[k, 0, pl.ds(low * CAP, span)] = moved[:span]
        for d in range(1, SIDE):
            slots[k, d - 1, pl.ds(low * CAP, span)] = moved[d * span : (d + 1) * span]

    def experts(k):
        def first(n, carry):
            taken = rows[k].reshape(SIDE * BLOCK, width)
            cols = pl.ds(pl.multiple_of(n * 256, 256), 256)
            both = jnp.dot(taken, w_in[:, cols], preferred_element_type=F32)
            gate, up = both[:, :128], both[:, 128:]
            value = gate / (1.0 + jnp.exp(-gate)) * up
            hidden[:, pl.ds(pl.multiple_of(n * 128, 128), 128)] = value.astype(BF16)
            return carry

        lax.fori_loop(0, tiles, first, 0, unroll=True)

    def project(k, h):
        def second(n, carry):
            cols = pl.ds(h * (width // 2) + n * 256, 256)
            value = jnp.dot(hidden[...], w_out[:, cols], preferred_element_type=F32)
            back[k, 0, :, cols] = value[:BLOCK].astype(BF16)
            for d in range(1, SIDE):
                part = value[d * BLOCK : (d + 1) * BLOCK]
                if d == 2 and k % 2:
                    part = part + pair_parts[k // 2, :, cols].astype(F32)
                parts[k, d - 1, :, cols] = part.astype(BF16)
            return carry

        for n in range(width // 512):
            second(n, 0)

    def choose(k):
        meta = dense[k, :, :, pl.ds(width, META)].reshape(SIDE * TOK, META)
        col = lax.broadcasted_iota(jnp.int32, (META, SIDE * BLOCK), 0)
        lane = lax.broadcasted_iota(jnp.int32, (META, SIDE * BLOCK), 1)
        mine = lane_expert(k, lane // BLOCK)

        def look(shift):
            pick = (col == mine + shift).astype(F32).astype(BF16)
            return jnp.dot(meta, pick, preferred_element_type=F32)

        token = lax.broadcasted_iota(jnp.int32, (SIDE * TOK, SIDE * BLOCK), 0)
        lane = lax.broadcasted_iota(jnp.int32, (SIDE * TOK, SIDE * BLOCK), 1)
        want = (lane % CAP + 1).astype(F32)
        near = (lane % BLOCK) // CAP == token // TOK
        match = (look(0) == want) & near
        high = jnp.where(match, look(EXPERTS), 0.0).astype(BF16)
        low = jnp.where(match, look(2 * EXPERTS), 0.0).astype(BF16)
        choice[k, 0], choice[k, 1] = high, low

    def merge(k, h):
        came = back[k, :, :, half(h)].reshape(SIDE * BLOCK, width // 2)
        total = jnp.dot(choice[k, 0], came, preferred_element_type=F32)
        total = total + jnp.dot(choice[k, 1], came, preferred_element_type=F32)
        for d in range(SIDE):
            part = total[d * TOK : (d + 1) * TOK]
            if d == 2 and k % 2:
                part = part + pair_merged[k // 2, :, half(h)].astype(F32)
            merged[k, d, :, half(h)] = part.astype(BF16)

    def gather_sum(k, h):
        total = merged[k, 0, :, half(h)].astype(F32)
        for d in near_hops(k ^ 1):
            total = total + spread[k, d - 1, :, half(h)].astype(F32)
        sums[k, :, half(h)] = total.astype(BF16)

    weights = [pltpu.make_async_copy(down_ref, w_out, w_sem.at[2 * tiles])]
    for n in range(tiles):
        for j, ref in enumerate((gate_ref, up_ref)):
            weights.append(
                pltpu.make_async_copy(
                    ref.at[:, pl.ds(n * 128, 128)],
                    w_in.at[:, pl.ds(n * 256 + j * 128, 128)],
                    w_sem.at[2 * n + j],
                )
            )

    for copy in weights:
        copy.start()

    @pl.when(stage == 0)
    def _():
        first_tile.wait()

    @pl.when(stage > 0)
    def _():
        relay.wait_recv()

    for copy in loads:
        copy.wait()
    prepare()
    start("d", 0, d_copies(0))
    for k in (2, 1, 3):
        start("z", k, {0: z_copy[k]})
    for k in (0, 2):
        back[k, 2] = jnp.zeros((BLOCK, width), BF16)

    def dense_on(k):
        arrive("z", k)
        start("d", k, d_copies(k))

    def send_rows(k, low, high):
        compact(k, low, high)
        start("f", (k, low), f_copies(k, low, high))

    def dispatch(k):
        arrive("d", k, (2,))
        if k % 2 == 0:
            start("zd", k, pair_copy(0, dense.at[k, 2], dense.at[k + 1, 2], k))
        else:
            arrive("zd", k - 1)
        arrive("d", k, (1, 3))
        send_rows(k, 1 if k % 2 == 0 else 0, SIDE)

    def arrive_rows(k, hops):
        arrive("f", (k, 0), hops)
        if k % 2 == 0:
            arrive("f", (k, 1), hops)

    def pass_rows(k):
        arrive_rows(k, (2,))
        start("zf", k, pair_copy(1, rows.at[k, 2], rows.at[k + 1, 2], k))

    def compute(k):
        arrive_rows(k, (1, 3))
        if k % 2:
            arrive("zf", k - 1)
        experts(k)
        for h in range(2):
            if k % 2:
                arrive("zrf", (k - 1, h))
            project(k, h)
            if k % 2 == 0:
                part, there = parts.at[k, 1, :, half(h)], pair_parts.at[k // 2, :, half(h)]
                start("zrf", (k, h), pair_copy(2, part, there, k, h))
            start("rf", (k, h), rf_copies(k, h))

    def combine(k, h):
        arrive("rf", (k, h))
        if k % 2:
            arrive("zrd", (k - 1, h))
        merge(k, h)
        if k % 2 == 0:
            part, there = merged.at[k, 2, :, half(h)], pair_merged.at[k // 2, :, half(h)]
            start("zrd", (k, h), pair_copy(3, part, there, k, h))
        start("rd", (k, h), rd_copies(k, h))

    def collect(k, h):
        arrive("rd", (k, h))
        gather_sum(k, h)
        if k:
            start("rz", (k, h), {0: rz_copy(k, h)})

    send_rows(0, 0, 1)
    dense_on(2)
    send_rows(2, 0, 1)
    dense_on(1)
    dispatch(0)
    dense_on(3)
    dispatch(2)
    dispatch(1)
    dispatch(3)
    for k in (0, 2, 1, 3):
        choose(k)
    for copy in weights:
        copy.wait()
    pass_rows(0)
    compute(0)
    pass_rows(2)
    compute(2)
    compute(1)
    combine(0, 0)
    combine(0, 1)
    compute(3)
    combine(2, 0)
    combine(2, 1)
    combine(1, 0)
    combine(3, 0)
    combine(1, 1)
    combine(3, 1)
    for h in range(2):
        for k in (0, 2, 3, 1):
            collect(k, h)
    for h in range(2):
        total = inputs[:, half(h)].astype(F32) + sums[0, :, half(h)].astype(F32)
        for k in (2, 3, 1):
            arrive("rz", (k, h))
            total = total + final[k, :, half(h)].astype(F32)
        out_ref[:, half(h)] = total.astype(BF16)
    for copies in steps.values():
        for copy in copies.values():
            copy.wait_send()

    @pl.when(stage < stages - 1)
    def _():
        relay.wait_send()


def run_layer(held, fresh, routes, gain, router, gate, up, down):
    tok, width = fresh.shape
    hid = gate.shape[1]
    vmem = pl.BlockSpec(memory_space=pltpu.VMEM)
    hbm = pl.BlockSpec(memory_space=pltpu.MemorySpace.HBM)
    dma = pltpu.SemaphoreType.DMA
    pairs = [dma((SIDE,)), dma((SIDE,))]
    wide = [dma((SIDE, 2 * SIDE)), dma((SIDE, 2 * SIDE))]
    grids = [dma((SIDE, SIDE)), dma((SIDE, SIDE))]
    return pl.pallas_call(
        moe_kernel,
        out_shape=jax.ShapeDtypeStruct((tok, width), BF16),
        in_specs=[hbm] * 8,
        out_specs=vmem,
        scratch_shapes=[
            pltpu.VMEM((tok, width), BF16),
            pltpu.VMEM(routes.shape, jnp.int32),
            pltpu.VMEM(gain.shape, F32),
            pltpu.VMEM(router.shape, BF16),
            pltpu.VMEM((SIDE, SIDE, tok, width + META), BF16),
            pltpu.VMEM((SIDE, SIDE - 1, BLOCK, width), BF16),
            pltpu.VMEM((SIDE, SIDE, BLOCK, width), BF16),
            pltpu.VMEM((SIDE, SIDE - 1, BLOCK, width), BF16),
            pltpu.VMEM((SIDE, SIDE, BLOCK, width), BF16),
            pltpu.VMEM((SIDE, SIDE, tok, width), BF16),
            pltpu.VMEM((SIDE, SIDE - 1, tok, width), BF16),
            pltpu.VMEM((SIDE, tok, width), BF16),
            pltpu.VMEM((SIDE, tok, width), BF16),
            pltpu.VMEM((2, BLOCK, width), BF16),
            pltpu.VMEM((2, tok, width), BF16),
            pltpu.VMEM((SIDE, 2, SIDE * tok, SIDE * BLOCK), BF16),
            pltpu.VMEM((SIDE * BLOCK, hid), BF16),
            pltpu.VMEM((width, 2 * hid), BF16),
            pltpu.VMEM((hid, width), BF16),
        ]
        + pairs + grids + wide + wide + wide + grids
        + wide + [dma((1,)), dma((1,)), dma((SIDE,)), dma((2 * (hid // 128) + 1,))],
        compiler_params=pltpu.CompilerParams(
            collective_id=0, has_side_effects=True, vmem_limit_bytes=58 * 1024 * 1024
        ),
        name="moe_relay",
    )(held, fresh, routes, gain, router, gate, up, down)


def per_device(held, fresh, routes, norm_gain, router, w_gate, w_up, w_down):
    out = run_layer(
        held[0], fresh, routes[0].T, norm_gain, router[0].T, w_gate[0, 0], w_up[0, 0], w_down[0, 0]
    )
    return out[None]


def solution(mesh):
    in_specs = (
        P("pipe", "expert", None),
        P("expert", None),
        P("pipe", "expert", None),
        P("pipe", None),
        P("pipe", None, None),
        P("pipe", "expert", None, None),
        P("pipe", "expert", None, None),
        P("pipe", "expert", None, None),
    )
    out_specs = P("pipe", "expert", None)
    return jax.shard_map(
        per_device, mesh=mesh, in_specs=in_specs, out_specs=out_specs, check_vma=False
    )
```

```python
import functools

import jax
import jax.numpy as jnp
from jax import lax
from jax.experimental import pallas as pl
from jax.experimental.pallas import tpu as pltpu
from jax.sharding import PartitionSpec as P

MESH = pl.DeviceIdType.MESH
SIDE = 4
EXPERTS = 8
CAP = 16
TOK = 32
META = 128
BLOCK = SIDE * CAP
F32 = jnp.float32
BF16 = jnp.bfloat16


def z_partner(z, k):
    return (z, z + 1 - 2 * (z % 2), (z + 2) % SIDE, 3 - z)[k]


def moe_kernel(
    held_ref, fresh_ref, routes_ref, gain_ref, router_ref, gate_ref, up_ref, down_ref, out_ref,
    inputs, chosen, gain, router, dense, slots, rows, parts, back, merged, spread, sums, final, pair_parts, pair_merged, choice, hidden, w_in, w_out,
    z_send, z_recv, d_send, d_recv, f_send, f_recv,
    rf_send, rf_recv, rd_send, rd_recv, rz_send, rz_recv, q_send, q_recv, p_send, p_recv, i_sem, w_sem,
):
    me = lax.axis_index("expert")
    stage, stages = lax.axis_index("pipe"), lax.axis_size("pipe")
    x, y, z = me // 16, (me // 4) % 4, me % 4
    width = fresh_ref.shape[1]
    tiles = gate_ref.shape[1] // 128

    def at(nx, ny, nz):
        return {"expert": nx * 16 + ny * 4 + nz}

    def along(axis, by):
        if axis == "x":
            return at((x + by + SIDE) % SIDE, y, z)
        return at(x, (y + by + SIDE) % SIDE, z)

    inner = ("x", "x", "y", "y")
    outer = ("y", "y", "x", "x")

    def section(by):
        return {"pipe": stage + by, "expert": me}

    loads = [
        pltpu.make_async_copy(ref, to, i_sem.at[n])
        for n, (ref, to) in enumerate(((routes_ref, chosen), (gain_ref, gain), (router_ref, router)))
    ]
    for copy in loads:
        copy.start()
    first_tile = pltpu.make_async_copy(fresh_ref, inputs, i_sem.at[3])

    @pl.when(stage == 0)
    def _():
        first_tile.start()

    barrier = pltpu.get_barrier_semaphore()

    @pl.when(stage < stages - 1)
    def _():
        pl.semaphore_signal(barrier, inc=1, device_id=section(1), device_id_type=MESH)

    @pl.when(stage > 0)
    def _():
        pl.semaphore_signal(barrier, inc=1, device_id=section(-1), device_id_type=MESH)

    for d in range(1, SIDE):
        for who in (along("x", d), along("y", d), at(x, y, z_partner(z, d))):
            pl.semaphore_signal(barrier, inc=1, device_id=who, device_id_type=MESH)
    before, after = (stage + stages - 1) // stages, (2 * stages - 2 - stage) // stages
    pl.semaphore_wait(barrier, 9 + before + after)

    def remote(src, dst, send, recv, who):
        return pltpu.make_async_remote_copy(
            src_ref=src, dst_ref=dst, send_sem=send, recv_sem=recv, device_id=who, device_id_type=MESH
        )

    relay = remote(held_ref, inputs, p_send.at[0], p_recv.at[0], section(1))

    @pl.when(stage < stages - 1)
    def _():
        relay.start()

    z_copy = {
        k: remote(dense.at[0, 0], dense.at[k, 0], z_send.at[k], z_recv.at[k], at(x, y, z_partner(z, k)))
        for k in (1, 2)
    }

    def d_copies(k):
        return {
            d: remote(dense.at[k, 0], dense.at[k, d], d_send.at[k, d], d_recv.at[k, d], along(inner[k], d))
            for d in near_hops(k)
        }

    def f_copies(k, low, high):
        span, lane = pl.ds(low * CAP, (high - low) * CAP), SIDE if low else 0
        return {
            d: remote(
                slots.at[k, d - 1, span], rows.at[k, d, span],
                f_send.at[k, lane + d], f_recv.at[k, lane + d], along(outer[k], d),
            )
            for d in near_hops(k)
        }

    def half(h):
        return pl.ds(h * (width // 2), width // 2)

    def rf_copies(k, h):
        return {
            d: remote(
                parts.at[k, d - 1, :, half(h)], back.at[k, d, :, half(h)],
                rf_send.at[k, h * SIDE + d], rf_recv.at[k, h * SIDE + d], along(outer[k], -d),
            )
            for d in near_hops(k ^ 1)
        }

    def rd_copies(k, h):
        return {
            d: remote(
                merged.at[k, d, :, half(h)], spread.at[k, d - 1, :, half(h)],
                rd_send.at[k, h * SIDE + d], rd_recv.at[k, h * SIDE + d], along(inner[k], -d),
            )
            for d in near_hops(k ^ 1)
        }

    def near_hops(k):
        return (2, 1, 3) if k % 2 == 0 else (1, 3)

    twin = at(x, y, z_partner(z, 1))

    def pair_copy(kind, src, dst, k, h=0):
        lane = h * SIDE + k // 2
        return {0: remote(src, dst, q_send.at[kind, lane], q_recv.at[kind, lane], twin)}

    def rz_copy(k, h):
        return remote(
            sums.at[k, :, half(h)], final.at[k, :, half(h)],
            rz_send.at[k, h], rz_recv.at[k, h], at(x, y, z_partner(z, k)),
        )

    steps = {}

    def start(name, k, copies):
        steps[name, k] = copies
        for copy in copies.values():
            copy.start()

    def arrive(name, k, hops=None):
        for d, copy in steps[name, k].items():
            if hops is None or d in hops:
                copy.wait_recv()

    def lane_expert(k, block):
        if outer[k] == "y":
            return 2 * x + ((y + block) % SIDE) // 2
        return 2 * ((x + block) % SIDE) + y // 2

    def prepare():
        values = inputs[...].astype(F32)
        mean_square = jnp.mean(values * values, axis=-1, keepdims=True)
        normed = (values * lax.rsqrt(mean_square + 1e-05) * gain[...]).astype(BF16)
        dense[0, 0, :, pl.ds(0, width)] = normed
        logits = lax.dot_general(
            router[...], normed, (((1,), (1,)), ((), ())), preferred_element_type=F32
        )
        ids = lax.broadcasted_iota(jnp.int32, (EXPERTS, TOK), 0)
        first, second = ids == chosen[0:1, :], ids == chosen[1:2, :]
        gap = jnp.sum(jnp.where(first, logits, 0.0), axis=0, keepdims=True) - jnp.sum(
            jnp.where(second, logits, 0.0), axis=0, keepdims=True
        )
        share_a, share_b = 1.0 / (1.0 + jnp.exp(-gap)), 1.0 / (1.0 + jnp.exp(gap))
        weight = jnp.where(first, share_a, 0.0) + jnp.where(second, share_b, 0.0)
        high = weight.astype(BF16).astype(F32)
        hit = jnp.where(first | second, 1.0, 0.0)
        here = lax.broadcasted_iota(jnp.int32, (TOK, TOK), 0)
        there = lax.broadcasted_iota(jnp.int32, (TOK, TOK), 1)
        upto = jnp.where(here <= there, 1.0, 0.0).astype(BF16)
        slot = hit * jnp.dot(hit.astype(BF16), upto, preferred_element_type=F32)
        table = jnp.concatenate(
            [slot, high, weight - high, jnp.zeros((META - 3 * EXPERTS, TOK), F32)], axis=0
        ).astype(BF16)
        same = jnp.where(here == there, 1.0, 0.0).astype(BF16)
        meta = lax.dot_general(same, table, (((1,), (1,)), ((), ())), preferred_element_type=F32)
        dense[0, 0, :, pl.ds(width, META)] = meta.astype(BF16)

    def compact(k, low, high):
        count, span = high - low, (high - low) * CAP
        tok = dense[k, low:high].reshape(count * TOK, width + META)
        meta = tok[:, width:]
        lane = lax.broadcasted_iota(jnp.int32, (SIDE * span, META), 0)
        col = lax.broadcasted_iota(jnp.int32, (SIDE * span, META), 1)
        pick = (col == lane_expert(k, lane // span)).astype(F32).astype(BF16)
        found = lax.dot_general(pick, meta, (((1,), (1,)), ((), ())), preferred_element_type=F32)
        lane = lax.broadcasted_iota(jnp.int32, (SIDE * span, count * TOK), 0)
        token = lax.broadcasted_iota(jnp.int32, (SIDE * span, count * TOK), 1)
        want = (lane % CAP + 1).astype(F32)
        near = (lane % span) // CAP == token // TOK
        placing = jnp.where((found == want) & near, 1.0, 0.0).astype(BF16)
        moved = jnp.dot(placing, tok[:, :width], preferred_element_type=F32).astype(BF16)
        rows[k, 0, pl.ds(low * CAP, span)] = moved[:span]
        for d in range(1, SIDE):
            slots[k, d - 1, pl.ds(low * CAP, span)] = moved[d * span : (d + 1) * span]

    def experts(k):
        def first(n, carry):
            taken = rows[k].reshape(SIDE * BLOCK, width)
            cols = pl.ds(pl.multiple_of(n * 256, 256), 256)
            both = jnp.dot(taken, w_in[:, cols], preferred_element_type=F32)
            gate, up = both[:, :128], both[:, 128:]
            value = gate / (1.0 + jnp.exp(-gate)) * up
            hidden[:, pl.ds(pl.multiple_of(n * 128, 128), 128)] = value.astype(BF16)
            return carry

        lax.fori_loop(0, tiles, first, 0, unroll=True)

    def project(k, h):
        def second(n, carry):
            cols = pl.ds(h * (width // 2) + n * 256, 256)
            value = jnp.dot(hidden[...], w_out[:, cols], preferred_element_type=F32)
            back[k, 0, :, cols] = value[:BLOCK].astype(BF16)
            for d in range(1, SIDE):
                part = value[d * BLOCK : (d + 1) * BLOCK]
                if d == 2 and k % 2:
                    part = part + pair_parts[k // 2, :, cols].astype(F32)
                parts[k, d - 1, :, cols] = part.astype(BF16)
            return carry

        for n in range(width // 512):
            second(n, 0)

    def choose(k):
        meta = dense[k, :, :, pl.ds(width, META)].reshape(SIDE * TOK, META)
        col = lax.broadcasted_iota(jnp.int32, (META, SIDE * BLOCK), 0)
        lane = lax.broadcasted_iota(jnp.int32, (META, SIDE * BLOCK), 1)
        mine = lane_expert(k, lane // BLOCK)

        def look(shift):
            pick = (col == mine + shift).astype(F32).astype(BF16)
            return jnp.dot(meta, pick, preferred_element_type=F32)

        token = lax.broadcasted_iota(jnp.int32, (SIDE * TOK, SIDE * BLOCK), 0)
        lane = lax.broadcasted_iota(jnp.int32, (SIDE * TOK, SIDE * BLOCK), 1)
        want = (lane % CAP + 1).astype(F32)
        near = (lane % BLOCK) // CAP == token // TOK
        match = (look(0) == want) & near
        high = jnp.where(match, look(EXPERTS), 0.0).astype(BF16)
        low = jnp.where(match, look(2 * EXPERTS), 0.0).astype(BF16)
        choice[k, 0], choice[k, 1] = high, low

    def merge(k, h):
        came = back[k, :, :, half(h)].reshape(SIDE * BLOCK, width // 2)
        total = jnp.dot(choice[k, 0], came, preferred_element_type=F32)
        total = total + jnp.dot(choice[k, 1], came, preferred_element_type=F32)
        for d in range(SIDE):
            part = total[d * TOK : (d + 1) * TOK]
            if d == 2 and k % 2:
                part = part + pair_merged[k // 2, :, half(h)].astype(F32)
            merged[k, d, :, half(h)] = part.astype(BF16)

    def gather_sum(k, h):
        total = merged[k, 0, :, half(h)].astype(F32)
        for d in near_hops(k ^ 1):
            total = total + spread[k, d - 1, :, half(h)].astype(F32)
        sums[k, :, half(h)] = total.astype(BF16)

    weights = [pltpu.make_async_copy(down_ref, w_out, w_sem.at[2 * tiles])]
    for n in range(tiles):
        for j, ref in enumerate((gate_ref, up_ref)):
            weights.append(
                pltpu.make_async_copy(
                    ref.at[:, pl.ds(n * 128, 128)],
                    w_in.at[:, pl.ds(n * 256 + j * 128, 128)],
                    w_sem.at[2 * n + j],
                )
            )

    for copy in weights:
        copy.start()

    @pl.when(stage == 0)
    def _():
        first_tile.wait()

    @pl.when(stage > 0)
    def _():
        relay.wait_recv()

    for copy in loads:
        copy.wait()
    prepare()
    start("d", 0, d_copies(0))
    for k in (2, 1):
        start("z", k, {0: z_copy[k]})
    for k in (0, 2):
        back[k, 2] = jnp.zeros((BLOCK, width), BF16)

    def dense_on(k):
        arrive("z", k)
        if k == 2:
            start("z", 3, {0: remote(dense.at[2, 0], dense.at[3, 0], z_send.at[3], z_recv.at[3], twin)})
        start("d", k, d_copies(k))

    def send_rows(k, low, high):
        compact(k, low, high)
        start("f", (k, low), f_copies(k, low, high))

    def dispatch(k):
        arrive("d", k, (2,))
        if k % 2 == 0:
            start("zd", k, pair_copy(0, dense.at[k, 2], dense.at[k + 1, 2], k))
        else:
            arrive("zd", k - 1)
        arrive("d", k, (1, 3))
        send_rows(k, 1 if k % 2 == 0 else 0, SIDE)

    def arrive_rows(k, hops):
        arrive("f", (k, 0), hops)
        if k % 2 == 0:
            arrive("f", (k, 1), hops)

    def pass_rows(k):
        arrive_rows(k, (2,))
        start("zf", k, pair_copy(1, rows.at[k, 2], rows.at[k + 1, 2], k))

    def compute(k):
        arrive_rows(k, (1, 3))
        if k % 2:
            arrive("zf", k - 1)
        experts(k)
        for h in range(2):
            if k % 2:
                arrive("zrf", (k - 1, h))
            project(k, h)
            if k % 2 == 0:
                part, there = parts.at[k, 1, :, half(h)], pair_parts.at[k // 2, :, half(h)]
                start("zrf", (k, h), pair_copy(2, part, there, k, h))
            start("rf", (k, h), rf_copies(k, h))

    def combine(k, h):
        arrive("rf", (k, h))
        if k % 2:
            arrive("zrd", (k - 1, h))
        merge(k, h)
        if k % 2 == 0:
            part, there = merged.at[k, 2, :, half(h)], pair_merged.at[k // 2, :, half(h)]
            start("zrd", (k, h), pair_copy(3, part, there, k, h))
        start("rd", (k, h), rd_copies(k, h))

    def collect(k, h):
        arrive("rd", (k, h))
        gather_sum(k, h)
        if k:
            start("rz", (k, h), {0: rz_copy(k, h)})

    send_rows(0, 0, 1)
    dense_on(2)
    dense_on(1)
    send_rows(2, 0, 1)
    dense_on(3)
    dispatch(0)
    choose(0)
    dispatch(2)
    choose(2)
    dispatch(1)
    choose(1)
    dispatch(3)
    for copy in weights:
        copy.wait()
    pass_rows(0)
    compute(0)
    pass_rows(2)
    compute(2)
    compute(1)
    choose(3)
    combine(0, 0)
    combine(0, 1)
    compute(3)
    combine(2, 0)
    combine(2, 1)
    combine(1, 0)
    combine(3, 0)
    collect(2, 0)
    collect(2, 1)
    combine(1, 1)
    combine(3, 1)
    collect(0, 0)
    collect(0, 1)
    for h in range(2):
        collect(3, h)
        collect(1, h)
    for h in range(2):
        total = inputs[:, half(h)].astype(F32) + sums[0, :, half(h)].astype(F32)
        for k in (2, 3, 1):
            arrive("rz", (k, h))
            total = total + final[k, :, half(h)].astype(F32)
        out_ref[:, half(h)] = total.astype(BF16)
    for copies in steps.values():
        for copy in copies.values():
            copy.wait_send()

    @pl.when(stage < stages - 1)
    def _():
        relay.wait_send()


def run_layer(held, fresh, routes, gain, router, gate, up, down):
    tok, width = fresh.shape
    hid = gate.shape[1]
    vmem = pl.BlockSpec(memory_space=pltpu.VMEM)
    hbm = pl.BlockSpec(memory_space=pltpu.MemorySpace.HBM)
    dma = pltpu.SemaphoreType.DMA
    pairs = [dma((SIDE,)), dma((SIDE,))]
    wide = [dma((SIDE, 2 * SIDE)), dma((SIDE, 2 * SIDE))]
    grids = [dma((SIDE, SIDE)), dma((SIDE, SIDE))]
    return pl.pallas_call(
        moe_kernel,
        out_shape=jax.ShapeDtypeStruct((tok, width), BF16),
        in_specs=[hbm] * 8,
        out_specs=vmem,
        scratch_shapes=[
            pltpu.VMEM((tok, width), BF16),
            pltpu.VMEM(routes.shape, jnp.int32),
            pltpu.VMEM(gain.shape, F32),
            pltpu.VMEM(router.shape, BF16),
            pltpu.VMEM((SIDE, SIDE, tok, width + META), BF16),
            pltpu.VMEM((SIDE, SIDE - 1, BLOCK, width), BF16),
            pltpu.VMEM((SIDE, SIDE, BLOCK, width), BF16),
            pltpu.VMEM((SIDE, SIDE - 1, BLOCK, width), BF16),
            pltpu.VMEM((SIDE, SIDE, BLOCK, width), BF16),
            pltpu.VMEM((SIDE, SIDE, tok, width), BF16),
            pltpu.VMEM((SIDE, SIDE - 1, tok, width), BF16),
            pltpu.VMEM((SIDE, tok, width), BF16),
            pltpu.VMEM((SIDE, tok, width), BF16),
            pltpu.VMEM((2, BLOCK, width), BF16),
            pltpu.VMEM((2, tok, width), BF16),
            pltpu.VMEM((SIDE, 2, SIDE * tok, SIDE * BLOCK), BF16),
            pltpu.VMEM((SIDE * BLOCK, hid), BF16),
            pltpu.VMEM((width, 2 * hid), BF16),
            pltpu.VMEM((hid, width), BF16),
        ]
        + pairs + grids + wide + wide + wide + grids
        + wide + [dma((1,)), dma((1,)), dma((SIDE,)), dma((2 * (hid // 128) + 1,))],
        compiler_params=pltpu.CompilerParams(
            collective_id=0, has_side_effects=True, vmem_limit_bytes=58 * 1024 * 1024
        ),
        name="moe_relay",
    )(held, fresh, routes, gain, router, gate, up, down)


def per_device(held, fresh, routes, norm_gain, router, w_gate, w_up, w_down):
    out = run_layer(
        held[0], fresh, routes[0].T, norm_gain, router[0].T, w_gate[0, 0], w_up[0, 0], w_down[0, 0]
    )
    return out[None]


def solution(mesh):
    in_specs = (
        P("pipe", "expert", None),
        P("expert", None),
        P("pipe", "expert", None),
        P("pipe", None),
        P("pipe", None, None),
        P("pipe", "expert", None, None),
        P("pipe", "expert", None, None),
        P("pipe", "expert", None, None),
    )
    out_specs = P("pipe", "expert", None)
    return jax.shard_map(
        per_device, mesh=mesh, in_specs=in_specs, out_specs=out_specs, check_vma=False
    )
```

```python
import functools

import jax
import jax.numpy as jnp
from jax import lax
from jax.experimental import pallas as pl
from jax.experimental.pallas import tpu as pltpu
from jax.sharding import PartitionSpec as P

MESH = pl.DeviceIdType.MESH
SIDE = 4
EXPERTS = 8
CAP = 16
TOK = 32
META = 128
BLOCK = SIDE * CAP
F32 = jnp.float32
BF16 = jnp.bfloat16


def z_partner(z, k):
    return (z, z + 1 - 2 * (z % 2), (z + 2) % SIDE, 3 - z)[k]


def moe_kernel(
    held_ref, fresh_ref, routes_ref, gain_ref, router_ref, gate_ref, up_ref, down_ref, out_ref,
    inputs, result, chosen, gain, router, dense, slots, rows, parts, back, merged, spread, sums, final, pair_parts, pair_merged, choice, hidden, w_in, w_out,
    z_send, z_recv, d_send, d_recv, f_send, f_recv,
    rf_send, rf_recv, rd_send, rd_recv, rz_send, rz_recv, q_send, q_recv, p_send, p_recv, o_sem, i_sem, w_sem,
):
    me = lax.axis_index("expert")
    stage, stages = lax.axis_index("pipe"), lax.axis_size("pipe")
    x, y, z = me // 16, (me // 4) % 4, me % 4
    width = fresh_ref.shape[1]
    tiles = gate_ref.shape[1] // 128

    def at(nx, ny, nz):
        return {"expert": nx * 16 + ny * 4 + nz}

    def along(axis, by):
        if axis == "x":
            return at((x + by + SIDE) % SIDE, y, z)
        return at(x, (y + by + SIDE) % SIDE, z)

    inner = ("x", "x", "y", "y")
    outer = ("y", "y", "x", "x")

    def section(by):
        return {"pipe": stage + by, "expert": me}

    loads = [
        pltpu.make_async_copy(ref, to, i_sem.at[n])
        for n, (ref, to) in enumerate(((routes_ref, chosen), (gain_ref, gain), (router_ref, router)))
    ]
    for copy in loads:
        copy.start()
    first_tile = pltpu.make_async_copy(fresh_ref, inputs, i_sem.at[3])

    @pl.when(stage == 0)
    def _():
        first_tile.start()

    barrier = pltpu.get_barrier_semaphore()

    @pl.when(stage < stages - 1)
    def _():
        pl.semaphore_signal(barrier, inc=1, device_id=section(1), device_id_type=MESH)

    @pl.when(stage > 0)
    def _():
        pl.semaphore_signal(barrier, inc=1, device_id=section(-1), device_id_type=MESH)

    for d in range(1, SIDE):
        for who in (along("x", d), along("y", d), at(x, y, z_partner(z, d))):
            pl.semaphore_signal(barrier, inc=1, device_id=who, device_id_type=MESH)
    before, after = (stage + stages - 1) // stages, (2 * stages - 2 - stage) // stages
    pl.semaphore_wait(barrier, 9 + before + after)

    def remote(src, dst, send, recv, who):
        return pltpu.make_async_remote_copy(
            src_ref=src, dst_ref=dst, send_sem=send, recv_sem=recv, device_id=who, device_id_type=MESH
        )

    relay = remote(held_ref, inputs, p_send.at[0], p_recv.at[0], section(1))

    @pl.when(stage < stages - 1)
    def _():
        relay.start()

    z_copy = {
        k: remote(dense.at[0, 0], dense.at[k, 0], z_send.at[k], z_recv.at[k], at(x, y, z_partner(z, k)))
        for k in (1, 2)
    }

    def d_copies(k):
        return {
            d: remote(dense.at[k, 0], dense.at[k, d], d_send.at[k, d], d_recv.at[k, d], along(inner[k], d))
            for d in near_hops(k)
        }

    def f_copies(k, low, high):
        span, lane = pl.ds(low * CAP, (high - low) * CAP), SIDE if low else 0
        return {
            d: remote(
                slots.at[k, d - 1, span], rows.at[k, d, span],
                f_send.at[k, lane + d], f_recv.at[k, lane + d], along(outer[k], d),
            )
            for d in near_hops(k)
        }

    def half(h):
        return pl.ds(h * (width // 2), width // 2)

    def rf_copies(k, h):
        return {
            d: remote(
                parts.at[k, d - 1, :, half(h)], back.at[k, d, :, half(h)],
                rf_send.at[k, h * SIDE + d], rf_recv.at[k, h * SIDE + d], along(outer[k], -d),
            )
            for d in near_hops(k ^ 1)
        }

    def rd_copies(k, h):
        return {
            d: remote(
                merged.at[k, d, :, half(h)], spread.at[k, d - 1, :, half(h)],
                rd_send.at[k, h * SIDE + d], rd_recv.at[k, h * SIDE + d], along(inner[k], -d),
            )
            for d in near_hops(k ^ 1)
        }

    def near_hops(k):
        return (2, 1, 3) if k % 2 == 0 else (1, 3)

    twin = at(x, y, z_partner(z, 1))

    def pair_copy(kind, src, dst, k, h=0):
        lane = h * SIDE + k // 2
        return {0: remote(src, dst, q_send.at[kind, lane], q_recv.at[kind, lane], twin)}

    def rz_copy(k, h):
        return remote(
            sums.at[k, :, half(h)], final.at[k, :, half(h)],
            rz_send.at[k, h], rz_recv.at[k, h], at(x, y, z_partner(z, k)),
        )

    steps = {}

    def start(name, k, copies):
        steps[name, k] = copies
        for copy in copies.values():
            copy.start()

    def arrive(name, k, hops=None):
        for d, copy in steps[name, k].items():
            if hops is None or d in hops:
                copy.wait_recv()

    def lane_expert(k, block):
        if outer[k] == "y":
            return 2 * x + ((y + block) % SIDE) // 2
        return 2 * ((x + block) % SIDE) + y // 2

    def prepare():
        values = inputs[...].astype(F32)
        mean_square = jnp.mean(values * values, axis=-1, keepdims=True)
        normed = (values * lax.rsqrt(mean_square + 1e-05) * gain[...]).astype(BF16)
        dense[0, 0, :, pl.ds(0, width)] = normed
        logits = lax.dot_general(
            router[...], normed, (((1,), (1,)), ((), ())), preferred_element_type=F32
        )
        ids = lax.broadcasted_iota(jnp.int32, (EXPERTS, TOK), 0)
        first, second = ids == chosen[0:1, :], ids == chosen[1:2, :]
        gap = jnp.sum(jnp.where(first, logits, 0.0), axis=0, keepdims=True) - jnp.sum(
            jnp.where(second, logits, 0.0), axis=0, keepdims=True
        )
        share_a, share_b = 1.0 / (1.0 + jnp.exp(-gap)), 1.0 / (1.0 + jnp.exp(gap))
        weight = jnp.where(first, share_a, 0.0) + jnp.where(second, share_b, 0.0)
        high = weight.astype(BF16).astype(F32)
        hit = jnp.where(first | second, 1.0, 0.0)
        here = lax.broadcasted_iota(jnp.int32, (TOK, TOK), 0)
        there = lax.broadcasted_iota(jnp.int32, (TOK, TOK), 1)
        upto = jnp.where(here <= there, 1.0, 0.0).astype(BF16)
        slot = hit * jnp.dot(hit.astype(BF16), upto, preferred_element_type=F32)
        table = jnp.concatenate(
            [slot, high, weight - high, jnp.zeros((META - 3 * EXPERTS, TOK), F32)], axis=0
        ).astype(BF16)
        same = jnp.where(here == there, 1.0, 0.0).astype(BF16)
        meta = lax.dot_general(same, table, (((1,), (1,)), ((), ())), preferred_element_type=F32)
        dense[0, 0, :, pl.ds(width, META)] = meta.astype(BF16)

    def compact(k, low, high):
        count, span = high - low, (high - low) * CAP
        tok = dense[k, low:high].reshape(count * TOK, width + META)
        meta = tok[:, width:]
        lane = lax.broadcasted_iota(jnp.int32, (SIDE * span, META), 0)
        col = lax.broadcasted_iota(jnp.int32, (SIDE * span, META), 1)
        pick = (col == lane_expert(k, lane // span)).astype(F32).astype(BF16)
        found = lax.dot_general(pick, meta, (((1,), (1,)), ((), ())), preferred_element_type=F32)
        lane = lax.broadcasted_iota(jnp.int32, (SIDE * span, count * TOK), 0)
        token = lax.broadcasted_iota(jnp.int32, (SIDE * span, count * TOK), 1)
        want = (lane % CAP + 1).astype(F32)
        near = (lane % span) // CAP == token // TOK
        placing = jnp.where((found == want) & near, 1.0, 0.0).astype(BF16)
        moved = jnp.dot(placing, tok[:, :width], preferred_element_type=F32).astype(BF16)
        rows[k, 0, pl.ds(low * CAP, span)] = moved[:span]
        for d in range(1, SIDE):
            slots[k, d - 1, pl.ds(low * CAP, span)] = moved[d * span : (d + 1) * span]

    def experts(k):
        def first(n, carry):
            taken = rows[k].reshape(SIDE * BLOCK, width)
            cols = pl.ds(pl.multiple_of(n * 256, 256), 256)
            both = jnp.dot(taken, w_in[:, cols], preferred_element_type=F32)
            gate, up = both[:, :128], both[:, 128:]
            value = gate / (1.0 + jnp.exp(-gate)) * up
            hidden[:, pl.ds(pl.multiple_of(n * 128, 128), 128)] = value.astype(BF16)
            return carry

        lax.fori_loop(0, tiles, first, 0, unroll=True)

    def project(k, h):
        def second(n, carry):
            cols = pl.ds(h * (width // 2) + n * 256, 256)
            value = jnp.dot(hidden[...], w_out[:, cols], preferred_element_type=F32)
            back[k, 0, :, cols] = value[:BLOCK].astype(BF16)
            for d in range(1, SIDE):
                part = value[d * BLOCK : (d + 1) * BLOCK]
                if d == 2 and k % 2:
                    part = part + pair_parts[k // 2, :, cols].astype(F32)
                parts[k, d - 1, :, cols] = part.astype(BF16)
            return carry

        for n in range(width // 512):
            second(n, 0)

    def choose(k):
        meta = dense[k, :, :, pl.ds(width, META)].reshape(SIDE * TOK, META)
        col = lax.broadcasted_iota(jnp.int32, (META, SIDE * BLOCK), 0)
        lane = lax.broadcasted_iota(jnp.int32, (META, SIDE * BLOCK), 1)
        mine = lane_expert(k, lane // BLOCK)

        def look(shift):
            pick = (col == mine + shift).astype(F32).astype(BF16)
            return jnp.dot(meta, pick, preferred_element_type=F32)

        token = lax.broadcasted_iota(jnp.int32, (SIDE * TOK, SIDE * BLOCK), 0)
        lane = lax.broadcasted_iota(jnp.int32, (SIDE * TOK, SIDE * BLOCK), 1)
        want = (lane % CAP + 1).astype(F32)
        near = (lane % BLOCK) // CAP == token // TOK
        match = (look(0) == want) & near
        high = jnp.where(match, look(EXPERTS), 0.0).astype(BF16)
        low = jnp.where(match, look(2 * EXPERTS), 0.0).astype(BF16)
        choice[k, 0], choice[k, 1] = high, low

    def merge(k, h):
        came = back[k, :, :, half(h)].reshape(SIDE * BLOCK, width // 2)
        total = jnp.dot(choice[k, 0], came, preferred_element_type=F32)
        total = total + jnp.dot(choice[k, 1], came, preferred_element_type=F32)
        for d in range(SIDE):
            part = total[d * TOK : (d + 1) * TOK]
            if d == 2 and k % 2:
                part = part + pair_merged[k // 2, :, half(h)].astype(F32)
            merged[k, d, :, half(h)] = part.astype(BF16)

    def gather_sum(k, h):
        total = merged[k, 0, :, half(h)].astype(F32)
        for d in near_hops(k ^ 1):
            total = total + spread[k, d - 1, :, half(h)].astype(F32)
        sums[k, :, half(h)] = total.astype(BF16)

    weights = [pltpu.make_async_copy(down_ref, w_out, w_sem.at[2 * tiles])]
    for n in range(tiles):
        for j, ref in enumerate((gate_ref, up_ref)):
            weights.append(
                pltpu.make_async_copy(
                    ref.at[:, pl.ds(n * 128, 128)],
                    w_in.at[:, pl.ds(n * 256 + j * 128, 128)],
                    w_sem.at[2 * n + j],
                )
            )

    @pl.when(stage == 0)
    def _():
        first_tile.wait()

    @pl.when(stage > 0)
    def _():
        relay.wait_recv()

    for copy in loads:
        copy.wait()
    prepare()
    start("d", 0, d_copies(0))
    for k in (2, 1):
        start("z", k, {0: z_copy[k]})
    for k in (0, 2):
        back[k, 2] = jnp.zeros((BLOCK, width), BF16)

    def dense_on(k):
        arrive("z", k)
        if k == 2:
            start("z", 3, {0: remote(dense.at[2, 0], dense.at[3, 0], z_send.at[3], z_recv.at[3], twin)})
        start("d", k, d_copies(k))

    def send_rows(k, low, high):
        compact(k, low, high)
        start("f", (k, low), f_copies(k, low, high))

    def dispatch(k):
        arrive("d", k, (2,))
        if k % 2 == 0:
            start("zd", k, pair_copy(0, dense.at[k, 2], dense.at[k + 1, 2], k))
        else:
            arrive("zd", k - 1)
        arrive("d", k, (1, 3))
        send_rows(k, 1 if k % 2 == 0 else 0, SIDE)

    def arrive_rows(k, hops):
        arrive("f", (k, 0), hops)
        if k % 2 == 0:
            arrive("f", (k, 1), hops)

    def pass_rows(k):
        arrive_rows(k, (2,))
        start("zf", k, pair_copy(1, rows.at[k, 2], rows.at[k + 1, 2], k))

    def compute(k):
        arrive_rows(k, (1, 3))
        if k % 2:
            arrive("zf", k - 1)
        experts(k)
        for h in range(2):
            if k % 2:
                arrive("zrf", (k - 1, h))
            project(k, h)
            if k % 2 == 0:
                part, there = parts.at[k, 1, :, half(h)], pair_parts.at[k // 2, :, half(h)]
                start("zrf", (k, h), pair_copy(2, part, there, k, h))
            start("rf", (k, h), rf_copies(k, h))

    def combine(k, h):
        arrive("rf", (k, h))
        if k % 2:
            arrive("zrd", (k - 1, h))
        merge(k, h)
        if k % 2 == 0:
            part, there = merged.at[k, 2, :, half(h)], pair_merged.at[k // 2, :, half(h)]
            start("zrd", (k, h), pair_copy(3, part, there, k, h))
        start("rd", (k, h), rd_copies(k, h))

    def collect(k, h):
        arrive("rd", (k, h))
        gather_sum(k, h)
        if k:
            start("rz", (k, h), {0: rz_copy(k, h)})

    send_rows(0, 0, 1)
    for copy in weights:
        copy.start()
    dense_on(2)
    dense_on(1)
    send_rows(2, 0, 1)
    dense_on(3)
    dispatch(0)
    choose(0)
    dispatch(2)
    choose(2)
    dispatch(1)
    choose(1)
    dispatch(3)
    for copy in weights:
        copy.wait()
    pass_rows(0)
    compute(0)
    pass_rows(2)
    compute(2)
    compute(1)
    choose(3)
    combine(0, 0)
    combine(0, 1)
    compute(3)
    combine(2, 0)
    combine(2, 1)
    combine(1, 0)
    combine(1, 1)
    combine(3, 0)
    collect(2, 0)
    collect(2, 1)
    combine(3, 1)
    collect(0, 0)
    collect(0, 1)
    for h in range(2):
        collect(3, h)
        collect(1, h)
    outputs = []
    for h in range(2):
        total = inputs[:, half(h)].astype(F32) + sums[0, :, half(h)].astype(F32)
        for k in (2, 3, 1):
            arrive("rz", (k, h))
            total = total + final[k, :, half(h)].astype(F32)
        result[:, half(h)] = total.astype(BF16)
        outputs.append(pltpu.make_async_copy(result.at[:, half(h)], out_ref.at[:, half(h)], o_sem.at[h]))
        outputs[h].start()
    for copies in steps.values():
        for copy in copies.values():
            copy.wait_send()
    for copy in outputs:
        copy.wait()

    @pl.when(stage < stages - 1)
    def _():
        relay.wait_send()


def run_layer(held, fresh, routes, gain, router, gate, up, down):
    tok, width = fresh.shape
    hid = gate.shape[1]
    hbm = pl.BlockSpec(memory_space=pltpu.MemorySpace.HBM)
    dma = pltpu.SemaphoreType.DMA
    pairs = [dma((SIDE,)), dma((SIDE,))]
    wide = [dma((SIDE, 2 * SIDE)), dma((SIDE, 2 * SIDE))]
    grids = [dma((SIDE, SIDE)), dma((SIDE, SIDE))]
    return pl.pallas_call(
        moe_kernel,
        out_shape=jax.ShapeDtypeStruct((tok, width), BF16),
        in_specs=[hbm] * 8,
        out_specs=hbm,
        scratch_shapes=[
            pltpu.VMEM((tok, width), BF16),
            pltpu.VMEM((tok, width), BF16),
            pltpu.VMEM(routes.shape, jnp.int32),
            pltpu.VMEM(gain.shape, F32),
            pltpu.VMEM(router.shape, BF16),
            pltpu.VMEM((SIDE, SIDE, tok, width + META), BF16),
            pltpu.VMEM((SIDE, SIDE - 1, BLOCK, width), BF16),
            pltpu.VMEM((SIDE, SIDE, BLOCK, width), BF16),
            pltpu.VMEM((SIDE, SIDE - 1, BLOCK, width), BF16),
            pltpu.VMEM((SIDE, SIDE, BLOCK, width), BF16),
            pltpu.VMEM((SIDE, SIDE, tok, width), BF16),
            pltpu.VMEM((SIDE, SIDE - 1, tok, width), BF16),
            pltpu.VMEM((SIDE, tok, width), BF16),
            pltpu.VMEM((SIDE, tok, width), BF16),
            pltpu.VMEM((2, BLOCK, width), BF16),
            pltpu.VMEM((2, tok, width), BF16),
            pltpu.VMEM((SIDE, 2, SIDE * tok, SIDE * BLOCK), BF16),
            pltpu.VMEM((SIDE * BLOCK, hid), BF16),
            pltpu.VMEM((width, 2 * hid), BF16),
            pltpu.VMEM((hid, width), BF16),
        ]
        + pairs + grids + wide + wide + wide + grids
        + wide + [dma((1,)), dma((1,)), dma((2,)), dma((SIDE,)), dma((2 * (hid // 128) + 1,))],
        compiler_params=pltpu.CompilerParams(
            collective_id=0, has_side_effects=True, vmem_limit_bytes=58 * 1024 * 1024
        ),
        name="moe_relay",
    )(held, fresh, routes, gain, router, gate, up, down)


def per_device(held, fresh, routes, norm_gain, router, w_gate, w_up, w_down):
    out = run_layer(
        held[0], fresh, routes[0].T, norm_gain, router[0].T, w_gate[0, 0], w_up[0, 0], w_down[0, 0]
    )
    return out[None]


def solution(mesh):
    in_specs = (
        P("pipe", "expert", None),
        P("expert", None),
        P("pipe", "expert", None),
        P("pipe", None),
        P("pipe", None, None),
        P("pipe", "expert", None, None),
        P("pipe", "expert", None, None),
        P("pipe", "expert", None, None),
    )
    out_specs = P("pipe", "expert", None)
    return jax.shard_map(
        per_device, mesh=mesh, in_specs=in_specs, out_specs=out_specs, check_vma=False
    )
```

```python
import functools

import jax
import jax.numpy as jnp
from jax import lax
from jax.experimental import pallas as pl
from jax.experimental.pallas import tpu as pltpu
from jax.sharding import PartitionSpec as P

MESH = pl.DeviceIdType.MESH
SIDE = 4
EXPERTS = 8
CAP = 16
TOK = 32
META = 128
BLOCK = SIDE * CAP
F32 = jnp.float32
BF16 = jnp.bfloat16


def z_partner(z, k):
    return (z, z + 1 - 2 * (z % 2), (z + 2) % SIDE, 3 - z)[k]


def moe_kernel(
    held_ref, fresh_ref, routes_ref, gain_ref, router_ref, gate_ref, up_ref, down_ref, out_ref,
    inputs, result, chosen, gain, router, dense, slots, rows, parts, back, merged, spread, sums, final, pair_parts, pair_merged, choice, hidden, w_in, w_out,
    z_send, z_recv, d_send, d_recv, f_send, f_recv,
    rf_send, rf_recv, rd_send, rd_recv, rz_send, rz_recv, q_send, q_recv, p_send, p_recv, o_sem, i_sem, w_sem,
):
    me = lax.axis_index("expert")
    stage, stages = lax.axis_index("pipe"), lax.axis_size("pipe")
    x, y, z = me // 16, (me // 4) % 4, me % 4
    width = fresh_ref.shape[1]
    tiles = gate_ref.shape[1] // 128

    def at(nx, ny, nz):
        return {"expert": nx * 16 + ny * 4 + nz}

    def along(axis, by):
        if axis == "x":
            return at((x + by + SIDE) % SIDE, y, z)
        return at(x, (y + by + SIDE) % SIDE, z)

    inner = ("x", "x", "y", "y")
    outer = ("y", "y", "x", "x")

    def section(by):
        return {"pipe": stage + by, "expert": me}

    loads = [
        pltpu.make_async_copy(ref, to, i_sem.at[n])
        for n, (ref, to) in enumerate(((routes_ref, chosen), (gain_ref, gain), (router_ref, router)))
    ]
    for copy in loads:
        copy.start()
    first_tile = pltpu.make_async_copy(fresh_ref, inputs, i_sem.at[3])

    @pl.when(stage == 0)
    def _():
        first_tile.start()

    barrier = pltpu.get_barrier_semaphore()

    @pl.when(stage < stages - 1)
    def _():
        pl.semaphore_signal(barrier, inc=1, device_id=section(1), device_id_type=MESH)

    @pl.when(stage > 0)
    def _():
        pl.semaphore_signal(barrier, inc=1, device_id=section(-1), device_id_type=MESH)

    for d in range(1, SIDE):
        for who in (along("x", d), along("y", d), at(x, y, z_partner(z, d))):
            pl.semaphore_signal(barrier, inc=1, device_id=who, device_id_type=MESH)
    before, after = (stage + stages - 1) // stages, (2 * stages - 2 - stage) // stages
    pl.semaphore_wait(barrier, 9 + before + after)

    def remote(src, dst, send, recv, who):
        return pltpu.make_async_remote_copy(
            src_ref=src, dst_ref=dst, send_sem=send, recv_sem=recv, device_id=who, device_id_type=MESH
        )

    relay = remote(held_ref, inputs, p_send.at[0], p_recv.at[0], section(1))

    @pl.when(stage < stages - 1)
    def _():
        relay.start()

    z_copy = {
        k: remote(dense.at[0, 0], dense.at[k, 0], z_send.at[k], z_recv.at[k], at(x, y, z_partner(z, k)))
        for k in (1, 2)
    }

    def d_copies(k):
        return {
            d: remote(dense.at[k, 0], dense.at[k, d], d_send.at[k, d], d_recv.at[k, d], along(inner[k], d))
            for d in near_hops(k)
        }

    def f_copies(k, low, high):
        span, lane = pl.ds(low * CAP, (high - low) * CAP), SIDE if low else 0
        return {
            d: remote(
                slots.at[k, d - 1, span], rows.at[k, d, span],
                f_send.at[k, lane + d], f_recv.at[k, lane + d], along(outer[k], d),
            )
            for d in near_hops(k)
        }

    def half(h):
        return pl.ds(h * (width // 2), width // 2)

    def rf_copies(k, h):
        return {
            d: remote(
                parts.at[k, d - 1, :, half(h)], back.at[k, d, :, half(h)],
                rf_send.at[k, h * SIDE + d], rf_recv.at[k, h * SIDE + d], along(outer[k], -d),
            )
            for d in near_hops(k ^ 1)
        }

    def rd_copies(k, h):
        return {
            d: remote(
                merged.at[k, d, :, half(h)], spread.at[k, d - 1, :, half(h)],
                rd_send.at[k, h * SIDE + d], rd_recv.at[k, h * SIDE + d], along(inner[k], -d),
            )
            for d in near_hops(k ^ 1)
        }

    def near_hops(k):
        return (2, 1, 3) if k % 2 == 0 else (1, 3)

    twin = at(x, y, z_partner(z, 1))

    def pair_copy(kind, src, dst, k, h=0):
        lane = h * SIDE + k // 2
        return {0: remote(src, dst, q_send.at[kind, lane], q_recv.at[kind, lane], twin)}

    def rz_copy(k, h):
        return remote(
            sums.at[k, :, half(h)], final.at[k, :, half(h)],
            rz_send.at[k, h], rz_recv.at[k, h], twin if k == 2 else at(x, y, z_partner(z, k)),
        )

    steps = {}

    def start(name, k, copies):
        steps[name, k] = copies
        for copy in copies.values():
            copy.start()

    def arrive(name, k, hops=None):
        for d, copy in steps[name, k].items():
            if hops is None or d in hops:
                copy.wait_recv()

    def lane_expert(k, block):
        if outer[k] == "y":
            return 2 * x + ((y + block) % SIDE) // 2
        return 2 * ((x + block) % SIDE) + y // 2

    def prepare():
        values = inputs[...].astype(F32)
        mean_square = jnp.mean(values * values, axis=-1, keepdims=True)
        normed = (values * lax.rsqrt(mean_square + 1e-05) * gain[...]).astype(BF16)
        dense[0, 0, :, pl.ds(0, width)] = normed
        logits = lax.dot_general(
            router[...], normed, (((1,), (1,)), ((), ())), preferred_element_type=F32
        )
        ids = lax.broadcasted_iota(jnp.int32, (EXPERTS, TOK), 0)
        first, second = ids == chosen[0:1, :], ids == chosen[1:2, :]
        gap = jnp.sum(jnp.where(first, logits, 0.0), axis=0, keepdims=True) - jnp.sum(
            jnp.where(second, logits, 0.0), axis=0, keepdims=True
        )
        share_a, share_b = 1.0 / (1.0 + jnp.exp(-gap)), 1.0 / (1.0 + jnp.exp(gap))
        weight = jnp.where(first, share_a, 0.0) + jnp.where(second, share_b, 0.0)
        high = weight.astype(BF16).astype(F32)
        hit = jnp.where(first | second, 1.0, 0.0)
        here = lax.broadcasted_iota(jnp.int32, (TOK, TOK), 0)
        there = lax.broadcasted_iota(jnp.int32, (TOK, TOK), 1)
        upto = jnp.where(here <= there, 1.0, 0.0).astype(BF16)
        slot = hit * jnp.dot(hit.astype(BF16), upto, preferred_element_type=F32)
        table = jnp.concatenate(
            [slot, high, weight - high, jnp.zeros((META - 3 * EXPERTS, TOK), F32)], axis=0
        ).astype(BF16)
        same = jnp.where(here == there, 1.0, 0.0).astype(BF16)
        meta = lax.dot_general(same, table, (((1,), (1,)), ((), ())), preferred_element_type=F32)
        dense[0, 0, :, pl.ds(width, META)] = meta.astype(BF16)

    def compact(k, low, high):
        count, span = high - low, (high - low) * CAP
        tok = dense[k, low:high].reshape(count * TOK, width + META)
        meta = tok[:, width:]
        lane = lax.broadcasted_iota(jnp.int32, (SIDE * span, META), 0)
        col = lax.broadcasted_iota(jnp.int32, (SIDE * span, META), 1)
        pick = (col == lane_expert(k, lane // span)).astype(F32).astype(BF16)
        found = lax.dot_general(pick, meta, (((1,), (1,)), ((), ())), preferred_element_type=F32)
        lane = lax.broadcasted_iota(jnp.int32, (SIDE * span, count * TOK), 0)
        token = lax.broadcasted_iota(jnp.int32, (SIDE * span, count * TOK), 1)
        want = (lane % CAP + 1).astype(F32)
        near = (lane % span) // CAP == token // TOK
        placing = jnp.where((found == want) & near, 1.0, 0.0).astype(BF16)
        moved = jnp.dot(placing, tok[:, :width], preferred_element_type=F32).astype(BF16)
        rows[k, 0, pl.ds(low * CAP, span)] = moved[:span]
        for d in range(1, SIDE):
            slots[k, d - 1, pl.ds(low * CAP, span)] = moved[d * span : (d + 1) * span]

    def experts(k):
        def first(n, carry):
            taken = rows[k].reshape(SIDE * BLOCK, width)
            cols = pl.ds(pl.multiple_of(n * 256, 256), 256)
            both = jnp.dot(taken, w_in[:, cols], preferred_element_type=F32)
            gate, up = both[:, :128], both[:, 128:]
            value = gate / (1.0 + jnp.exp(-gate)) * up
            hidden[:, pl.ds(pl.multiple_of(n * 128, 128), 128)] = value.astype(BF16)
            return carry

        lax.fori_loop(0, tiles, first, 0, unroll=True)

    def project(k, h):
        def second(n, carry):
            cols = pl.ds(h * (width // 2) + n * 256, 256)
            value = jnp.dot(hidden[...], w_out[:, cols], preferred_element_type=F32)
            back[k, 0, :, cols] = value[:BLOCK].astype(BF16)
            for d in range(1, SIDE):
                part = value[d * BLOCK : (d + 1) * BLOCK]
                if d == 2 and k % 2:
                    part = part + pair_parts[k // 2, :, cols].astype(F32)
                parts[k, d - 1, :, cols] = part.astype(BF16)
            return carry

        for n in range(width // 512):
            second(n, 0)

    def choose(k):
        meta = dense[k, :, :, pl.ds(width, META)].reshape(SIDE * TOK, META)
        col = lax.broadcasted_iota(jnp.int32, (META, SIDE * BLOCK), 0)
        lane = lax.broadcasted_iota(jnp.int32, (META, SIDE * BLOCK), 1)
        mine = lane_expert(k, lane // BLOCK)

        def look(shift):
            pick = (col == mine + shift).astype(F32).astype(BF16)
            return jnp.dot(meta, pick, preferred_element_type=F32)

        token = lax.broadcasted_iota(jnp.int32, (SIDE * TOK, SIDE * BLOCK), 0)
        lane = lax.broadcasted_iota(jnp.int32, (SIDE * TOK, SIDE * BLOCK), 1)
        want = (lane % CAP + 1).astype(F32)
        near = (lane % BLOCK) // CAP == token // TOK
        match = (look(0) == want) & near
        high = jnp.where(match, look(EXPERTS), 0.0).astype(BF16)
        low = jnp.where(match, look(2 * EXPERTS), 0.0).astype(BF16)
        choice[k, 0], choice[k, 1] = high, low

    def merge(k, h):
        came = back[k, :, :, half(h)].reshape(SIDE * BLOCK, width // 2)
        total = jnp.dot(choice[k, 0], came, preferred_element_type=F32)
        total = total + jnp.dot(choice[k, 1], came, preferred_element_type=F32)
        for d in range(SIDE):
            part = total[d * TOK : (d + 1) * TOK]
            if d == 2 and k % 2:
                part = part + pair_merged[k // 2, :, half(h)].astype(F32)
            merged[k, d, :, half(h)] = part.astype(BF16)

    def gather_sum(k, h):
        total = merged[k, 0, :, half(h)].astype(F32)
        for d in near_hops(k ^ 1):
            total = total + spread[k, d - 1, :, half(h)].astype(F32)
        if k == 3:
            total = total + final[2, :, half(h)].astype(F32)
        sums[k, :, half(h)] = total.astype(BF16)

    weights = [pltpu.make_async_copy(down_ref, w_out, w_sem.at[2 * tiles])]
    for n in range(tiles):
        for j, ref in enumerate((gate_ref, up_ref)):
            weights.append(
                pltpu.make_async_copy(
                    ref.at[:, pl.ds(n * 128, 128)],
                    w_in.at[:, pl.ds(n * 256 + j * 128, 128)],
                    w_sem.at[2 * n + j],
                )
            )

    @pl.when(stage == 0)
    def _():
        first_tile.wait()

    @pl.when(stage > 0)
    def _():
        relay.wait_recv()

    for copy in loads:
        copy.wait()
    prepare()
    start("d", 0, d_copies(0))
    for k in (2, 1):
        start("z", k, {0: z_copy[k]})
    for k in (0, 2):
        back[k, 2] = jnp.zeros((BLOCK, width), BF16)

    def dense_on(k):
        arrive("z", k)
        if k == 2:
            start("z", 3, {0: remote(dense.at[2, 0], dense.at[3, 0], z_send.at[3], z_recv.at[3], twin)})
        start("d", k, d_copies(k))

    def send_rows(k, low, high):
        compact(k, low, high)
        start("f", (k, low), f_copies(k, low, high))

    def dispatch(k):
        arrive("d", k, (2,))
        if k % 2 == 0:
            start("zd", k, pair_copy(0, dense.at[k, 2], dense.at[k + 1, 2], k))
        else:
            arrive("zd", k - 1)
        arrive("d", k, (1, 3))
        send_rows(k, 1 if k % 2 == 0 else 0, SIDE)

    def arrive_rows(k, hops):
        arrive("f", (k, 0), hops)
        if k % 2 == 0:
            arrive("f", (k, 1), hops)

    def pass_rows(k):
        arrive_rows(k, (2,))
        start("zf", k, pair_copy(1, rows.at[k, 2], rows.at[k + 1, 2], k))

    def compute(k):
        arrive_rows(k, (1, 3))
        if k % 2:
            arrive("zf", k - 1)
        experts(k)
        for h in range(2):
            if k % 2:
                arrive("zrf", (k - 1, h))
            project(k, h)
            if k % 2 == 0:
                part, there = parts.at[k, 1, :, half(h)], pair_parts.at[k // 2, :, half(h)]
                start("zrf", (k, h), pair_copy(2, part, there, k, h))
            start("rf", (k, h), rf_copies(k, h))

    def combine(k, h):
        arrive("rf", (k, h))
        if k % 2:
            arrive("zrd", (k - 1, h))
        merge(k, h)
        if k % 2 == 0:
            part, there = merged.at[k, 2, :, half(h)], pair_merged.at[k // 2, :, half(h)]
            start("zrd", (k, h), pair_copy(3, part, there, k, h))
        start("rd", (k, h), rd_copies(k, h))

    def collect(k, h):
        arrive("rd", (k, h))
        if k == 3:
            arrive("rz", (2, h))
        gather_sum(k, h)
        if k:
            start("rz", (k, h), {0: rz_copy(k, h)})

    send_rows(0, 0, 1)
    for copy in weights:
        copy.start()
    dense_on(2)
    dense_on(1)
    send_rows(2, 0, 1)
    dense_on(3)
    dispatch(0)
    choose(0)
    dispatch(2)
    choose(2)
    dispatch(1)
    choose(1)
    dispatch(3)
    for copy in weights:
        copy.wait()
    pass_rows(0)
    compute(0)
    pass_rows(2)
    compute(2)
    compute(1)
    choose(3)
    combine(0, 0)
    combine(0, 1)
    compute(3)
    combine(2, 0)
    combine(2, 1)
    combine(1, 0)
    combine(1, 1)
    combine(3, 0)
    collect(2, 0)
    collect(2, 1)
    combine(3, 1)
    collect(0, 0)
    collect(0, 1)
    for h in range(2):
        collect(3, h)
        collect(1, h)
    outputs = []
    for h in range(2):
        total = inputs[:, half(h)].astype(F32) + sums[0, :, half(h)].astype(F32)
        for k in (3, 1):
            arrive("rz", (k, h))
            total = total + final[k, :, half(h)].astype(F32)
        result[:, half(h)] = total.astype(BF16)
        outputs.append(pltpu.make_async_copy(result.at[:, half(h)], out_ref.at[:, half(h)], o_sem.at[h]))
        outputs[h].start()
    for copies in steps.values():
        for copy in copies.values():
            copy.wait_send()
    for copy in outputs:
        copy.wait()

    @pl.when(stage < stages - 1)
    def _():
        relay.wait_send()


def run_layer(held, fresh, routes, gain, router, gate, up, down):
    tok, width = fresh.shape
    hid = gate.shape[1]
    hbm = pl.BlockSpec(memory_space=pltpu.MemorySpace.HBM)
    dma = pltpu.SemaphoreType.DMA
    pairs = [dma((SIDE,)), dma((SIDE,))]
    wide = [dma((SIDE, 2 * SIDE)), dma((SIDE, 2 * SIDE))]
    grids = [dma((SIDE, SIDE)), dma((SIDE, SIDE))]
    return pl.pallas_call(
        moe_kernel,
        out_shape=jax.ShapeDtypeStruct((tok, width), BF16),
        in_specs=[hbm] * 8,
        out_specs=hbm,
        scratch_shapes=[
            pltpu.VMEM((tok, width), BF16),
            pltpu.VMEM((tok, width), BF16),
            pltpu.VMEM(routes.shape, jnp.int32),
            pltpu.VMEM(gain.shape, F32),
            pltpu.VMEM(router.shape, BF16),
            pltpu.VMEM((SIDE, SIDE, tok, width + META), BF16),
            pltpu.VMEM((SIDE, SIDE - 1, BLOCK, width), BF16),
            pltpu.VMEM((SIDE, SIDE, BLOCK, width), BF16),
            pltpu.VMEM((SIDE, SIDE - 1, BLOCK, width), BF16),
            pltpu.VMEM((SIDE, SIDE, BLOCK, width), BF16),
            pltpu.VMEM((SIDE, SIDE, tok, width), BF16),
            pltpu.VMEM((SIDE, SIDE - 1, tok, width), BF16),
            pltpu.VMEM((SIDE, tok, width), BF16),
            pltpu.VMEM((SIDE, tok, width), BF16),
            pltpu.VMEM((2, BLOCK, width), BF16),
            pltpu.VMEM((2, tok, width), BF16),
            pltpu.VMEM((SIDE, 2, SIDE * tok, SIDE * BLOCK), BF16),
            pltpu.VMEM((SIDE * BLOCK, hid), BF16),
            pltpu.VMEM((width, 2 * hid), BF16),
            pltpu.VMEM((hid, width), BF16),
        ]
        + pairs + grids + wide + wide + wide + grids
        + wide + [dma((1,)), dma((1,)), dma((2,)), dma((SIDE,)), dma((2 * (hid // 128) + 1,))],
        compiler_params=pltpu.CompilerParams(
            collective_id=0, has_side_effects=True, vmem_limit_bytes=58 * 1024 * 1024
        ),
        name="moe_relay",
    )(held, fresh, routes, gain, router, gate, up, down)


def per_device(held, fresh, routes, norm_gain, router, w_gate, w_up, w_down):
    out = run_layer(
        held[0], fresh, routes[0].T, norm_gain, router[0].T, w_gate[0, 0], w_up[0, 0], w_down[0, 0]
    )
    return out[None]


def solution(mesh):
    in_specs = (
        P("pipe", "expert", None),
        P("expert", None),
        P("pipe", "expert", None),
        P("pipe", None),
        P("pipe", None, None),
        P("pipe", "expert", None, None),
        P("pipe", "expert", None, None),
        P("pipe", "expert", None, None),
    )
    out_specs = P("pipe", "expert", None)
    return jax.shard_map(
        per_device, mesh=mesh, in_specs=in_specs, out_specs=out_specs, check_vma=False
    )
```
